32 devices in a mesh: dp: 4 (over y, core), ctx: 8 (over z, x).
Axes of the slice: x: 2, y: 2, z: 4, core: 2. Of those that a mesh axis runs over, the one named last changes fastest.
Arguments:
- hidden_in: bfloat16 [4, 2048, 3584], P('dp', 'ctx'), may hold values from -6 to 6
- norm_gain: float32 [3584], replicated, may hold values from 0.1 to 1.9
- w_query: bfloat16 [3584, 1792], P(('dp', 'ctx')), may hold values from -3 to 3
- w_key: bfloat16 [3584, 256], P(('dp', 'ctx')), may hold values from -3 to 3
- value_weight: bfloat16 [3584, 256], P(('dp', 'ctx')), may hold values from -0.09375 to 0.09375
- marker_key_weight: bfloat16 [3584, 256], P(('dp', 'ctx')), may hold values from -0.09375 to 0.09375
- marker_value_weight: bfloat16 [3584, 256], P(('dp', 'ctx')), may hold values from -0.09375 to 0.09375
- ratio_level: int32 [4, 8], P('dp', 'ctx'), may hold values from 0 to 3, as said below
- hist_len: int32 [4], P('dp'), may hold values from 1025 to 2048, as said below
Outputs:
- attended: bfloat16 [4, 2048, 1792], P('dp', 'ctx')
The draws below stay inside these ranges and needn't reach their ends.
Inputs may be any that keep to these rules, and one draw needn't show every extreme that they name: `ratio_level`: each history has a span at level 0 and a span at level 3, so some span fills all 64 beacon slots. `hist_len`: one history of every draw is used to its full length 2048.
All inputs are finite; a program needn't handle non-finite values.
Results may differ from the reference program's by a relative error of at most 0.0069.
Values may be sent and summed in bfloat16 or wider, within the bound.
A program may use at most 128 MiB of HBM per device.

```python
import math
import jax
import jax.numpy as jnp
from jax import lax

MODEL_WIDTH = 3584
QUERY_HEADS = 14
KEY_VALUE_HEADS = 2
HEAD_SIZE = 128
TOK_DEV = 256
BEA = 64
NCH = 8
L = 2048
B = 4
N_CTX = 8


def linked_baseline(key):
    return jax.random.normal(jax.random.fold_in(key, 11), (MODEL_WIDTH, KEY_VALUE_HEADS * HEAD_SIZE), jnp.float32) / math.sqrt(MODEL_WIDTH)


def draw_w_key(key, part):
    return linked_baseline(key).astype(jnp.bfloat16)


def draw_w_query(key, part):
    noise_draw = jax.random.normal(jax.random.fold_in(key, 12), (MODEL_WIDTH, QUERY_HEADS * HEAD_SIZE), jnp.float32) / math.sqrt(MODEL_WIDTH)
    result = 0.5 * noise_draw
    return result.astype(jnp.bfloat16)


def draw_ratio_level(key, part):
    levels = jax.random.randint(key, (B, NCH), 0, 4, jnp.int32)
    first_pick = jax.random.randint(jax.random.fold_in(key, 21), (B,), 0, NCH, jnp.int32)
    other_pick = (first_pick + 1 + jax.random.randint(jax.random.fold_in(key, 22), (B,), 0, NCH - 1, jnp.int32)) % NCH
    column = jnp.arange(NCH, dtype=jnp.int32)[None, :]
    levels = jnp.where(column == first_pick[:, None], 0, levels)
    levels = jnp.where(column == other_pick[:, None], 3, levels)
    return levels.astype(jnp.int32)


def draw_hist_len(key, part):
    lengths = L - jax.random.randint(key, (B,), 0, L // 2, jnp.int32)
    full_row = jax.random.randint(jax.random.fold_in(key, 31), (), 0, B, jnp.int32)
    lengths = jnp.where(jnp.arange(B, dtype=jnp.int32) == full_row, L, lengths)
    return lengths.astype(jnp.int32)


def block_scale(key, extent, split, least, high):
    factor_of, own = 1.0, jax.random.fold_in(key, 6)
    for dim, blocks in split:
        heights = jnp.exp(jax.random.uniform(jax.random.fold_in(own, dim), (blocks,), jnp.float32, least / len(split), high / len(split)))
        factor_of = factor_of * jnp.repeat(heights, extent[dim] // blocks).reshape([-1 if axis == dim else 1 for axis in range(len(extent))])
    return factor_of


def gaussian(own_key, dims, width, most, split=(), kind=jnp.bfloat16):
    entries = width * jax.random.normal(own_key, dims, jnp.float32)
    if split:
        entries = entries * block_scale(own_key, dims, split, -0.22, 0.18)
    return jnp.clip(entries, -most, most).astype(kind)


def setup_inputs(seed: int = 0) -> dict:
    splits = jax.random.split(jax.random.key(seed), 10)
    hidden_in = gaussian(splits[0], (B, L, MODEL_WIDTH), 1.0, 6.0, ((0, 4), (1, 8)))
    norm_gain = jnp.clip(1.0 + 0.18 * jax.random.normal(splits[1], (MODEL_WIDTH,), jnp.float32), 0.1, 1.9)
    w_query = draw_w_query(jax.random.fold_in(splits[9], 71), 0)
    w_key = draw_w_key(jax.random.fold_in(splits[9], 71), 0)
    value_weight = gaussian(splits[4], (MODEL_WIDTH, KEY_VALUE_HEADS * HEAD_SIZE), MODEL_WIDTH ** -0.5, 0.09375, ((0, 32),))
    marker_key_weight = gaussian(splits[5], (MODEL_WIDTH, KEY_VALUE_HEADS * HEAD_SIZE), MODEL_WIDTH ** -0.5, 0.09375, ((0, 32),))
    marker_value_weight = gaussian(splits[6], (MODEL_WIDTH, KEY_VALUE_HEADS * HEAD_SIZE), MODEL_WIDTH ** -0.5, 0.09375, ((0, 32),))
    ratio_level = draw_ratio_level(jax.random.fold_in(splits[9], 71), 0)
    hist_len = draw_hist_len(jax.random.fold_in(splits[9], 71), 0)
    return {"hidden_in": hidden_in, "norm_gain": norm_gain, "w_query": w_query, "w_key": w_key, "value_weight": value_weight, "marker_key_weight": marker_key_weight, "marker_value_weight": marker_value_weight, "ratio_level": ratio_level, "hist_len": hist_len}


eps_norm = 1e-06
negative_filler = -1e+30

def norm_rows(tokens, norm_gain):
    values = tokens.astype(jnp.float32)
    factor = lax.rsqrt(lax.optimization_barrier(jnp.mean(values * values, axis=-1, keepdims=True)) + eps_norm)
    return (values * factor * norm_gain).astype(jnp.bfloat16)

def window_table(span_level, begin_offset, length, token_rows, marker_slot_count):
    stride = (4 * jnp.power(2, span_level)).astype(jnp.int32)
    live_count = token_rows // stride
    slot_ids = lax.broadcasted_iota(jnp.int32, (marker_slot_count, token_rows), 0)
    pos_ids = lax.broadcasted_iota(jnp.int32, (marker_slot_count, token_rows), 1)
    inside = (pos_ids // stride == slot_ids) & (slot_ids < live_count) & (begin_offset + pos_ids < length)
    slot_col = jnp.arange(marker_slot_count, dtype=jnp.int32)
    live_slot = (slot_col < live_count) & (begin_offset + slot_col * stride < length)
    return (inside, live_slot)

def pool_rows(inside, normed):
    window_sum = jnp.dot(inside.astype(jnp.bfloat16), normed, preferred_element_type=jnp.float32)
    window_size = lax.optimization_barrier(jnp.sum(inside.astype(jnp.float32), axis=1))
    return (window_sum / jnp.maximum(window_size, 1.0)[:, None]).astype(jnp.bfloat16)

def reference(hidden_in, norm_gain, w_query, w_key, value_weight, marker_key_weight, marker_value_weight, ratio_level, hist_len):
    token_rows = TOK_DEV
    marker_slot_count = BEA
    segment_ranges = N_CTX
    query_group_count = QUERY_HEADS // KEY_VALUE_HEADS
    score_scale = 1.0 / math.sqrt(HEAD_SIZE)

    def one_history(history):
        tokens, levels, length = history
        normed = norm_rows(tokens, norm_gain)
        query_matrix = jnp.dot(normed, w_query, preferred_element_type=jnp.float32).astype(jnp.bfloat16)
        key_matrix = jnp.dot(normed, w_key, preferred_element_type=jnp.float32).astype(jnp.bfloat16)
        value_matrix = jnp.dot(normed, value_weight, preferred_element_type=jnp.float32).astype(jnp.bfloat16)

        def pool_span(span_id):
            block = lax.dynamic_slice_in_dim(normed, span_id * token_rows, token_rows, 0)
            inside, live_slot = window_table(levels[span_id], span_id * token_rows, length, token_rows, marker_slot_count)
            return (pool_rows(inside, block), live_slot)
        pooled, live_slot = lax.map(pool_span, jnp.arange(segment_ranges, dtype=jnp.int32))
        pooled = pooled.reshape(segment_ranges * marker_slot_count, MODEL_WIDTH)
        live_slot = live_slot.reshape(segment_ranges * marker_slot_count)
        marker_key_rows = jnp.dot(pooled, marker_key_weight, preferred_element_type=jnp.float32).astype(jnp.bfloat16)
        marker_value_rows = jnp.dot(pooled, marker_value_weight, preferred_element_type=jnp.float32).astype(jnp.bfloat16)
        marker_key_rows = marker_key_rows.reshape(segment_ranges * marker_slot_count, KEY_VALUE_HEADS, HEAD_SIZE)
        marker_value_rows = marker_value_rows.reshape(segment_ranges * marker_slot_count, KEY_VALUE_HEADS, HEAD_SIZE)
        owner = jnp.arange(segment_ranges * marker_slot_count, dtype=jnp.int32) // marker_slot_count

        def attend_span(span_id):
            begin_offset = span_id * token_rows
            segment_query = lax.dynamic_slice_in_dim(query_matrix, begin_offset, token_rows, 0).astype(jnp.float32)
            segment_query = segment_query.reshape(token_rows, KEY_VALUE_HEADS, query_group_count, HEAD_SIZE)
            segment_key = lax.dynamic_slice_in_dim(key_matrix, begin_offset, token_rows, 0).reshape(token_rows, KEY_VALUE_HEADS, HEAD_SIZE)
            segment_value = lax.dynamic_slice_in_dim(value_matrix, begin_offset, token_rows, 0).reshape(token_rows, KEY_VALUE_HEADS, HEAD_SIZE)
            all_keys = jnp.concatenate([marker_key_rows, segment_key], axis=0).astype(jnp.float32)
            all_values = jnp.concatenate([marker_value_rows, segment_value], axis=0).astype(jnp.float32)
            positions = jnp.arange(token_rows, dtype=jnp.int32)
            seen_beacon = live_slot & (owner < span_id)
            seen_raw = (positions[None, :] <= positions[:, None]) & (begin_offset + positions[None, :] < length)
            visible = jnp.concatenate([jnp.broadcast_to(seen_beacon[None, :], (token_rows, segment_ranges * marker_slot_count)), seen_raw], axis=1)
            scores = jnp.einsum('tkgd,skd->kgts', segment_query, all_keys) * score_scale
            scores = jnp.where(visible, scores, negative_filler)
            top_score = lax.optimization_barrier(jnp.max(scores, axis=-1, keepdims=True))
            weights = jnp.where(visible, jnp.exp(scores - top_score), 0.0)
            weight_sum = lax.optimization_barrier(jnp.sum(weights, axis=-1))
            rounded = weights.astype(jnp.bfloat16).astype(jnp.float32)
            weighted = jnp.einsum('kgts,skd->kgtd', rounded, all_values)
            result = weighted / jnp.where(weight_sum > 0, weight_sum, 1.0)[..., None]
            result = result.transpose(2, 0, 1, 3).reshape(token_rows, QUERY_HEADS * HEAD_SIZE)
            valid = begin_offset + positions < length
            return jnp.where(valid[:, None], result, 0.0).astype(jnp.bfloat16)
        output = lax.map(attend_span, jnp.arange(segment_ranges, dtype=jnp.int32))
        return output.reshape(segment_ranges * token_rows, QUERY_HEADS * HEAD_SIZE)
    return lax.map(one_history, (hidden_in, ratio_level, hist_len))
```

```python
import functools
import math

import jax
import jax.numpy as jnp
from jax import lax
from jax.experimental import pallas as pl
from jax.experimental.pallas import tpu as pltpu
from jax.sharding import PartitionSpec as P

QUERY_HEADS = 14
KEY_VALUE_HEADS = 2
HEAD_SIZE = 128


eps_norm = 1e-06
negative_filler = -1e30


def norm_rows(tokens, norm_gain):
    values = tokens.astype(jnp.float32)
    factor = lax.rsqrt(jnp.mean(values * values, axis=-1, keepdims=True) + eps_norm)
    return (values * factor * norm_gain).astype(jnp.bfloat16)


def window_table(span_level, begin_offset, length, token_rows, marker_slot_count):
    stride = (4 * jnp.power(2, span_level)).astype(jnp.int32)
    live_count = token_rows // stride
    slot_ids = lax.broadcasted_iota(jnp.int32, (marker_slot_count, token_rows), 0)
    pos_ids = lax.broadcasted_iota(jnp.int32, (marker_slot_count, token_rows), 1)
    inside = (
        (pos_ids // stride == slot_ids)
        & (slot_ids < live_count)
        & (begin_offset + pos_ids < length)
    )
    slot_col = jnp.arange(marker_slot_count, dtype=jnp.int32)
    live_slot = (slot_col < live_count) & (begin_offset + slot_col * stride < length)
    return (inside, live_slot)


def pool_rows(inside, normed):
    window_sum = jnp.dot(inside.astype(jnp.bfloat16), normed, preferred_element_type=jnp.float32)
    window_size = jnp.sum(inside.astype(jnp.float32), axis=1)
    return (window_sum / jnp.maximum(window_size, 1.0)[:, None]).astype(jnp.bfloat16)


def raw_attention(query_matrix, key_matrix, value_matrix, begin_offset, length, score_scale):
    token_rows = key_matrix.shape[0]
    scores = (
        jnp.einsum("kgtd,skd->kgts", query_matrix, key_matrix, preferred_element_type=jnp.float32)
        * score_scale
    )
    positions = jnp.arange(token_rows, dtype=jnp.int32)
    visible = (positions[None, :] <= positions[:, None]) & (
        begin_offset + positions[None, :] < length
    )
    scores = jnp.where(visible, scores, negative_filler)
    top_score = jnp.max(scores, axis=-1)
    weights = jnp.where(visible, jnp.exp(scores - top_score[..., None]), 0.0)
    weight_sum = jnp.sum(weights, axis=-1)
    weighted = jnp.einsum(
        "kgts,skd->kgtd",
        weights.astype(jnp.bfloat16),
        value_matrix,
        preferred_element_type=jnp.float32,
    )
    return (top_score, weight_sum, weighted)


def beacon_update(
    carry_state,
    query_matrix,
    limit,
    marker_key_rows,
    marker_value_rows,
    beacon_live,
    marker_slot_count,
    score_scale,
):
    row_total = marker_key_rows.shape[0]
    span_of = jnp.arange(row_total, dtype=jnp.int32) // marker_slot_count
    visible = (beacon_live > 0) & (span_of < limit)

    def compute(state):
        running, weight_sum, weighted = state
        scores = (
            jnp.einsum(
                "kgtd,skd->kgts", query_matrix, marker_key_rows, preferred_element_type=jnp.float32
            )
            * score_scale
        )
        scores = jnp.where(visible, scores, negative_filler)
        new_top = jnp.maximum(running, jnp.max(scores, axis=-1))
        weights = jnp.where(visible, jnp.exp(scores - new_top[..., None]), 0.0)
        added = jnp.einsum(
            "kgts,skd->kgtd",
            weights.astype(jnp.bfloat16),
            marker_value_rows,
            preferred_element_type=jnp.float32,
        )
        return (new_top, jnp.sum(weights, axis=-1), added)

    def unchanged(state):
        return state

    return lax.cond(jnp.any(visible), compute, unchanged, carry_state)


def on_device(
    hidden_in,
    norm_gain,
    w_query,
    w_key,
    value_weight,
    marker_key_weight,
    marker_value_weight,
    ratio_level,
    hist_len,
):
    token_rows = hidden_in.shape[1]
    marker_slot_count = token_rows // 4
    my_span = lax.axis_index("ctx")
    begin_offset = my_span * token_rows
    length = hist_len[0]
    query_group_count = QUERY_HEADS // KEY_VALUE_HEADS
    score_scale = 1.0 / math.sqrt(HEAD_SIZE)
    normed = norm_rows(hidden_in[0], norm_gain)
    inside, live_slot = window_table(
        ratio_level[0, 0], begin_offset, length, token_rows, marker_slot_count
    )
    pooled = pool_rows(inside, normed)
    local_part = (
        lax.all_gather(w_query, "ctx", axis=0, tiled=True),
        lax.all_gather(w_key, "ctx", axis=0, tiled=True),
        lax.all_gather(value_weight, "ctx", axis=0, tiled=True),
        lax.all_gather(marker_key_weight, "ctx", axis=0, tiled=True),
        lax.all_gather(marker_value_weight, "ctx", axis=0, tiled=True),
    )
    segment_list = (
        lax.all_gather(local_part[0], "dp", axis=0, tiled=True),
        lax.all_gather(local_part[1], "dp", axis=0, tiled=True),
        lax.all_gather(local_part[2], "dp", axis=0, tiled=True),
        lax.all_gather(local_part[3], "dp", axis=0, tiled=True),
        lax.all_gather(local_part[4], "dp", axis=0, tiled=True),
    )
    flattened_query = jnp.dot(normed, segment_list[0], preferred_element_type=jnp.float32).astype(
        jnp.bfloat16
    )
    query_matrix = flattened_query.reshape(
        token_rows, KEY_VALUE_HEADS, query_group_count, HEAD_SIZE
    ).transpose(1, 2, 0, 3)
    key_matrix = (
        jnp.dot(normed, segment_list[1], preferred_element_type=jnp.float32)
        .astype(jnp.bfloat16)
        .reshape(token_rows, KEY_VALUE_HEADS, HEAD_SIZE)
    )
    value_matrix = (
        jnp.dot(normed, segment_list[2], preferred_element_type=jnp.float32)
        .astype(jnp.bfloat16)
        .reshape(token_rows, KEY_VALUE_HEADS, HEAD_SIZE)
    )
    marker_key_rows = jnp.dot(pooled, segment_list[3], preferred_element_type=jnp.float32).astype(
        jnp.bfloat16
    )
    marker_value_rows = jnp.dot(pooled, segment_list[4], preferred_element_type=jnp.float32).astype(
        jnp.bfloat16
    )
    raw_top, raw_sum, raw_weighted = raw_attention(
        query_matrix, key_matrix, value_matrix, begin_offset, length, score_scale
    )
    halved_rows = token_rows // 2
    first_q = query_matrix[:, :, :halved_rows]
    second_q = query_matrix[:, :, halved_rows:]
    empty_state = (
        jnp.full((KEY_VALUE_HEADS, query_group_count, halved_rows), negative_filler, jnp.float32),
        jnp.zeros((KEY_VALUE_HEADS, query_group_count, halved_rows), jnp.float32),
        jnp.zeros((KEY_VALUE_HEADS, query_group_count, halved_rows, HEAD_SIZE), jnp.float32),
    )
    segment_list = (
        lax.all_gather(marker_key_rows, "ctx", axis=0, tiled=True),
        lax.all_gather(marker_value_rows, "ctx", axis=0, tiled=True),
        lax.all_gather(live_slot.astype(jnp.bfloat16), "ctx", axis=0, tiled=True),
    )
    segment_keys = segment_list[0].reshape(-1, KEY_VALUE_HEADS, HEAD_SIZE)
    segment_values = segment_list[1].reshape(-1, KEY_VALUE_HEADS, HEAD_SIZE)
    first_state = beacon_update(
        empty_state,
        first_q,
        my_span,
        segment_keys,
        segment_values,
        segment_list[2],
        marker_slot_count,
        score_scale,
    )
    second_state = beacon_update(
        empty_state,
        second_q,
        my_span,
        segment_keys,
        segment_values,
        segment_list[2],
        marker_slot_count,
        score_scale,
    )
    first_state, second_state = (first_state, second_state)
    beacon_top = jnp.concatenate([first_state[0], second_state[0]], axis=2)
    beacon_sum = jnp.concatenate([first_state[1], second_state[1]], axis=2)
    beacon_weighted = jnp.concatenate([first_state[2], second_state[2]], axis=2)
    joint_top = jnp.maximum(raw_top, beacon_top)
    raw_factor = jnp.exp(raw_top - joint_top)
    beacon_factor = jnp.exp(beacon_top - joint_top)
    weight_sum = raw_sum * raw_factor + beacon_sum * beacon_factor
    weighted = raw_weighted * raw_factor[..., None] + beacon_weighted * beacon_factor[..., None]
    result = weighted / jnp.where(weight_sum > 0, weight_sum, 1.0)[..., None]
    result = result.transpose(2, 0, 1, 3).reshape(token_rows, QUERY_HEADS * HEAD_SIZE)
    valid = begin_offset + jnp.arange(token_rows, dtype=jnp.int32) < length
    result = jnp.where(valid[:, None], result, 0.0).astype(jnp.bfloat16)
    return result[None]


GROUP = QUERY_HEADS // KEY_VALUE_HEADS
PIECES = 4 + GROUP
GROUPS = (PIECES + 1) // 2
AHEAD = 3
Y_FIRST = (PIECES - 2, PIECES - 1)
FLOWS = [(p, 0) for p in range(PIECES)] + [(p, 1) for p in Y_FIRST]
STRIPS = 4
MESH = pl.DeviceIdType.MESH


def sublayer_kernel(
    n_dp,
    n_ctx,
    length_ref,
    level_ref,
    hidden_hbm,
    gain_ref,
    wq_ref,
    wk_ref,
    wv_ref,
    mk_ref,
    mv_ref,
    out_ref,
    hidden,
    levels,
    weights_buf,
    normed,
    pooled,
    beacons,
    live_bias,
    kv_buf,
    q_buf,
    span_bias,
    raw_bias,
    made_out,
    own_sem,
    load_sem,
    xs,
    xr,
    zu,
    zd,
    zr,
    ys,
    yr,
    cs,
    cr,
    hs,
    hr,
    ls,
    lr,
    bs,
    br,
    os_,
    or_,
    keep_sem,
):
    tokens = hidden_hbm.shape[0]
    rows = wq_ref.shape[0]
    slots = tokens // 4
    n_z = n_ctx // 2
    pair = 2 * slots
    dp = lax.axis_index("dp")
    ctx = lax.axis_index("ctx")
    z, x = ctx // 2, lax.rem(ctx, 2)
    other_x = 1 - x
    x_peer = (dp, z * 2 + other_x)
    y_dp = lax.rem(dp + n_dp // 2, n_dp)
    y_peer = (y_dp, ctx)
    mate = (dp + 1 - 2 * lax.rem(dp, 2), ctx)
    has_up, has_down = z + 1 < n_z, z > 0
    z_up = (dp, lax.rem(z + 1, n_z) * 2 + x)
    z_down = (dp, lax.rem(z + n_z - 1, n_z) * 2 + x)

    barrier = pltpu.get_barrier_semaphore()

    def greet(peer):
        pl.semaphore_signal(barrier, inc=1, device_id=peer, device_id_type=MESH)

    for peer in (x_peer, y_peer, mate):
        greet(peer)

    @pl.when(has_up)
    def _():
        greet(z_up)

    @pl.when(has_down)
    def _():
        greet(z_down)

    def remote(source, target, send, recv, peer):
        return pltpu.make_async_remote_copy(
            src_ref=source,
            dst_ref=target,
            send_sem=send,
            recv_sem=recv,
            device_id=peer,
            device_id_type=MESH,
        )

    strip = tokens // STRIPS

    def load_copy(i):
        part = pl.ds(i * strip, strip)
        return pltpu.make_async_copy(
            hidden_hbm.at[part, :], hidden.at[0, part, :], load_sem.at[i]
        )

    for i in range(STRIPS):
        load_copy(i).start()

    def piece_source(p, head):
        if p < 4:
            ref = (mk_ref, mv_ref, wk_ref, wv_ref)[p]
            column = head * HEAD_SIZE
        else:
            ref = wq_ref
            column = (head * GROUP + p - 4) * HEAD_SIZE
        return ref.at[:, pl.ds(pl.multiple_of(column, HEAD_SIZE), HEAD_SIZE)]

    def piece_rows(p, start, count):
        return weights_buf.at[
            p // 2,
            pl.ds(pl.multiple_of(start * rows, 16), count * rows),
            pl.ds((p % 2) * HEAD_SIZE, HEAD_SIZE),
        ]

    me = dp * n_ctx + ctx

    def own_copy(p):
        return pltpu.make_async_copy(piece_source(p, x), piece_rows(p, me, 1), own_sem.at[p])

    def x_copy(p):
        return remote(
            piece_source(p, other_x), piece_rows(p, me, 1), xs.at[p], xr.at[p], x_peer
        )

    for p in range(PIECES):
        own_copy(p).start()

    for m in range(1, n_z):

        @pl.when(z < m)
        def _():
            beacons[m * pair : (m + 1) * pair, :] = jnp.zeros(
                (pair, 2 * HEAD_SIZE), jnp.bfloat16
            )
            live_bias[m] = jnp.full((8, pair), negative_filler, jnp.float32)

    levels[x] = jnp.broadcast_to(level_ref[0, 0], (8, 128))
    length = length_ref[0]

    pl.semaphore_wait(
        barrier, 3 + has_up.astype(jnp.int32) + has_down.astype(jnp.int32)
    )

    def z_copy(f, source, step):
        p, column = FLOWS[f]
        block = piece_rows(p, (dp, y_dp)[column] * n_ctx + source * 2, 2)
        sends = zu if step > 0 else zd
        peer = z_up if step > 0 else z_down
        return remote(block, block, sends.at[f, source], zr.at[f, source], peer)

    def y_copy(p, source):
        block = piece_rows(p, dp * n_ctx + source * 2, 2)
        return remote(block, block, ys.at[p, source], yr.at[p, source], y_peer)

    def c_copy(p, which):
        block = piece_rows(p, (dp, y_dp)[which] * n_ctx, n_ctx)
        return remote(block, block, cs.at[p, which], cr.at[p, which], mate)

    def begin(p):
        x_copy(p).wait_recv()
        own_copy(p).wait()
        y_copy(p, z).start()

    def launch(f):
        p, column = FLOWS[f]
        if column == 1:
            y_copy(p, z).wait_recv()
        elif p not in Y_FIRST:
            begin(p)

        @pl.when(has_up)
        def _():
            z_copy(f, z, 1).start()

        @pl.when(has_down)
        def _():
            z_copy(f, z, -1).start()

    def relay(f, d):
        p, column = FLOWS[f]
        spread = column == 0 and p not in Y_FIRST

        @pl.when(z - d >= 0)
        def _():
            z_copy(f, z - d, 1).wait_recv()
            if spread:
                y_copy(p, z - d).start()

            @pl.when(has_up)
            def _():
                z_copy(f, z - d, 1).start()

        @pl.when(z + d < n_z)
        def _():
            z_copy(f, z + d, -1).wait_recv()
            if spread:
                y_copy(p, z + d).start()

            @pl.when(has_down)
            def _():
                z_copy(f, z + d, -1).start()

        if d == n_z - 1:
            c_copy(p, column).start()

    def tick(t):
        for d in range(1, n_z):
            f = t - d + 1
            if 0 <= f < len(FLOWS):
                relay(f, d)
        if t + AHEAD < len(FLOWS):
            launch(t + AHEAD)

    def y_arrived(p):
        if p not in Y_FIRST:
            for source in range(n_z):
                y_copy(p, source).wait_recv()
            c_copy(p, 1).start()

    def arrived(p):
        c_copy(p, 0).wait_recv()
        c_copy(p, 1).wait_recv()

    def z_sent(f):
        for source in range(n_z):

            @pl.when(has_up & (source <= z))
            def _():
                z_copy(f, source, 1).wait_send()

            @pl.when(has_down & (source >= z))
            def _():
                z_copy(f, source, -1).wait_send()

    def hidden_copy(i):
        part = pl.ds(i * strip, strip)
        return remote(
            hidden_hbm.at[part, :], hidden.at[1, part, :], hs.at[i], hr.at[i], x_peer
        )

    level_copy = remote(levels.at[x], levels.at[x], ls.at[0], lr.at[0], x_peer)

    def beacon_copies(m):
        keys = beacons.at[pl.ds(pl.multiple_of(m * pair, 128), pair), :]
        bias = live_bias.at[m]
        return (
            remote(keys, keys, bs.at[0, m], br.at[0, m], z_up),
            remote(bias, bias, bs.at[1, m], br.at[1, m], z_up),
        )

    def head_columns(head, j):
        return pl.ds(pl.multiple_of((head * GROUP + j) * HEAD_SIZE, HEAD_SIZE), HEAD_SIZE)

    def out_copy(j):
        return remote(
            made_out.at[1, j], out_ref.at[:, head_columns(x, j)], os_.at[j], or_.at[j], x_peer
        )

    def in_copy(j):
        return remote(
            made_out.at[1, j],
            out_ref.at[:, head_columns(other_x, j)],
            os_.at[j],
            or_.at[j],
            x_peer,
        )

    def keep_copy(j):
        return pltpu.make_async_copy(
            made_out.at[0, j], out_ref.at[:, head_columns(x, j)], keep_sem.at[j]
        )

    for p in range(PIECES):
        x_copy(p).start()
    level_copy.start()
    for i in range(STRIPS):
        hidden_copy(i).start()

    gain = gain_ref[...][None, :]

    def norm_strip(i, which, slot):
        def body(k, carry):
            part = pl.ds(pl.multiple_of(i * strip + k * 16, 16), 16)
            values = hidden[which, part, :].astype(jnp.float32)
            factor = lax.rsqrt(jnp.mean(values * values, axis=-1, keepdims=True) + eps_norm)
            normed[slot, part, :] = (values * factor * gain).astype(jnp.bfloat16)
            return carry

        lax.fori_loop(0, strip // 16, body, 0)

    def norm_own(i):
        load_copy(i).wait()
        norm_strip(i, 0, x)

    def norm_other(i):
        hidden_copy(i).wait_recv()
        norm_strip(i, 1, other_x)

    lane = lax.broadcasted_iota(jnp.int32, (1, pair), 1)
    slot_id = lax.rem(lane, slots)
    sub = lane // slots

    def stride_of(level):
        return jnp.where(
            level == 0, 4, jnp.where(level == 1, 8, jnp.where(level == 2, 16, 32))
        )

    def own_live():
        level = jnp.where(sub == 0, levels[0, 0:1, :], levels[1, 0:1, :])
        stride = stride_of(level)
        owner = 2 * z + sub
        live = (slot_id * stride < tokens) & (owner * tokens + slot_id * stride < length)
        live_bias[z] = jnp.broadcast_to(jnp.where(live, 0.0, negative_filler), (8, pair))

    def mask_far():
        for s in range(2):
            for m in range(n_z):
                seen = (2 * m + sub) < (2 * z + s)
                span_bias[s, :, m * pair : (m + 1) * pair] = jnp.where(
                    seen, live_bias[m], negative_filler
                )

    def mask_near():
        for s in range(2):
            row_id = lax.broadcasted_iota(jnp.int32, (tokens, tokens), 0)
            col_id = lax.broadcasted_iota(jnp.int32, (tokens, tokens), 1)
            seen = (col_id <= row_id) & ((z * 2 + s) * tokens + col_id < length)
            raw_bias[s] = jnp.where(seen, 0.0, negative_filler)

    def pool(s):
        span = z * 2 + s
        level = jnp.broadcast_to(levels[s, 0:1, :], (slots, 128))
        stride = stride_of(level)
        slot = lax.broadcasted_iota(jnp.int32, (slots, 128), 0)
        parts = []
        for b in range(tokens // 128):
            pos = lax.broadcasted_iota(jnp.int32, (slots, 128), 1) + b * 128
            inside = (
                (pos >= slot * stride)
                & (pos < (slot + 1) * stride)
                & (span * tokens + pos < length)
            )
            parts.append(jnp.where(inside, 1.0, 0.0))
        inside = jnp.concatenate(parts, axis=1)
        scale = 1.0 / jnp.maximum(jnp.sum(inside, axis=1, keepdims=True), 1.0)
        table = inside.astype(jnp.bfloat16)
        width = normed.shape[2] // 4

        def body(i, carry):
            cols = pl.ds(pl.multiple_of(i * width, 128), width)
            total = jnp.dot(table, normed[s, :, cols], preferred_element_type=jnp.float32)
            pooled[pl.ds(pl.multiple_of(s * slots, slots), slots), cols] = (
                total * scale
            ).astype(jnp.bfloat16)
            return carry

        lax.fori_loop(0, 4, body, 0)

    def project_kv(s):
        kv_buf[s] = jnp.dot(
            normed[s], weights_buf[1], preferred_element_type=jnp.float32
        ).astype(jnp.bfloat16)

    def project_query(s, g):
        result = jnp.dot(
            normed[s], weights_buf[g], preferred_element_type=jnp.float32
        ).astype(jnp.bfloat16)
        q_buf[s, 2 * (g - 2)] = result[:, :HEAD_SIZE]
        q_buf[s, 2 * (g - 2) + 1] = result[:, HEAD_SIZE:]

    def project_last(s):
        q_buf[s, GROUP - 1] = jnp.dot(
            normed[s], weights_buf[GROUPS - 1, :, :HEAD_SIZE], preferred_element_type=jnp.float32
        ).astype(jnp.bfloat16)

    def make_beacons():
        made = jnp.dot(pooled[...], weights_buf[0], preferred_element_type=jnp.float32)
        beacons[pl.ds(pl.multiple_of(z * pair, 128), pair), :] = made.astype(jnp.bfloat16)

        @pl.when(has_up)
        def _():
            for copy in beacon_copies(z):
                copy.start()

    def pass_beacons():
        for d in range(1, n_z):

            @pl.when(z - d >= 0)
            def _():
                for copy in beacon_copies(z - d):
                    copy.wait_recv()

                    @pl.when(has_up)
                    def _():
                        copy.start()

    factor = math.log2(math.e) / math.sqrt(HEAD_SIZE)
    contract = (((1,), (1,)), ((), ()))

    def attend(s, j, which, width):
        query = q_buf[s, j]
        far = lax.dot_general(
            query, beacons[:width, :HEAD_SIZE], contract, preferred_element_type=jnp.float32
        )
        near = lax.dot_general(
            query, kv_buf[s, :, :HEAD_SIZE], contract, preferred_element_type=jnp.float32
        )
        far = far * factor + span_bias[s, 0:1, :width]
        near = near * factor + raw_bias[s]
        top = jnp.maximum(
            jnp.max(far, axis=1, keepdims=True), jnp.max(near, axis=1, keepdims=True)
        )
        far = jnp.exp2(far - top)
        near = jnp.exp2(near - top)
        total = jnp.sum(far, axis=1, keepdims=True) + jnp.sum(near, axis=1, keepdims=True)
        mixed = jnp.dot(
            far.astype(jnp.bfloat16),
            beacons[:width, HEAD_SIZE:],
            preferred_element_type=jnp.float32,
        ) + jnp.dot(
            near.astype(jnp.bfloat16),
            kv_buf[s, :, HEAD_SIZE:],
            preferred_element_type=jnp.float32,
        )
        position = (z * 2 + s) * tokens + lax.broadcasted_iota(jnp.int32, (tokens, 1), 0)
        scale = jnp.where(position < length, 1.0 / total, 0.0)
        made_out[which, j] = (mixed * scale).astype(jnp.bfloat16)

    def heads(first, last):
        def step(j, carry):
            for which, s in ((1, other_x), (0, x)):

                @pl.when(z == 0)
                def _():
                    attend(s, j, which, pair)

                @pl.when(z > 0)
                def _():
                    attend(s, j, which, n_z * pair)

                (keep_copy, out_copy)[which](j).start()
            return carry

        lax.fori_loop(first, last, step, 0)

    for f in range(AHEAD):
        launch(f)
    for i in range(STRIPS):
        norm_own(i)
    for p in Y_FIRST:
        begin(p)
    tick(0)
    pool(x)
    mask_near()
    tick(1)
    tick(2)
    norm_other(0)
    tick(3)
    tick(4)
    y_arrived(0)
    y_arrived(1)
    level_copy.wait_recv()
    own_live()
    norm_other(1)
    tick(5)
    y_arrived(2)
    tick(6)
    y_arrived(3)
    norm_other(2)
    tick(7)
    y_arrived(4)
    arrived(2)
    arrived(3)
    project_kv(x)
    tick(8)
    y_arrived(5)
    tick(9)
    arrived(4)
    arrived(5)
    project_query(x, 2)
    y_arrived(6)
    tick(10)
    norm_other(3)
    pool(other_x)
    arrived(0)
    arrived(1)
    make_beacons()
    y_arrived(7)
    tick(11)
    project_kv(other_x)
    project_query(other_x, 2)
    pass_beacons()
    tick(12)
    arrived(6)
    arrived(7)
    project_query(x, 3)
    tick(13)
    project_query(other_x, 3)
    tick(14)
    y_arrived(8)
    mask_far()
    heads(0, 4)
    arrived(8)
    arrived(9)
    project_query(x, 4)
    project_query(other_x, 4)
    heads(4, 6)
    arrived(10)
    project_last(x)
    project_last(other_x)
    heads(6, 7)
    for j in range(GROUP):
        keep_copy(j).wait()
        out_copy(j).wait_send()
        in_copy(j).wait_recv()
    for p in range(PIECES):
        x_copy(p).wait_send()
        for source in range(n_z):
            if p not in Y_FIRST:
                y_copy(p, source).wait_send()
        if p in Y_FIRST:
            y_copy(p, z).wait_send()
        c_copy(p, 0).wait_send()
        c_copy(p, 1).wait_send()
    for f in range(len(FLOWS)):
        z_sent(f)
    for i in range(STRIPS):
        hidden_copy(i).wait_send()
    level_copy.wait_send()
    for m in range(n_z):

        @pl.when(has_up & (m <= z))
        def _():
            for copy in beacon_copies(m):
                copy.wait_send()


def on_device_paired(
    n_dp,
    n_ctx,
    hidden_in,
    norm_gain,
    w_query,
    w_key,
    value_weight,
    marker_key_weight,
    marker_value_weight,
    ratio_level,
    hist_len,
):
    tokens, width = hidden_in.shape[1:]
    slots = tokens // 4
    n_z = n_ctx // 2
    flows = len(FLOWS)
    dma = pltpu.SemaphoreType.DMA
    vmem = pl.BlockSpec(memory_space=pltpu.VMEM)
    smem = pl.BlockSpec(memory_space=pltpu.SMEM)
    hbm = pl.BlockSpec(memory_space=pl.ANY)
    bf16 = jnp.bfloat16
    result = pl.pallas_call(
        functools.partial(sublayer_kernel, n_dp, n_ctx),
        out_shape=jax.ShapeDtypeStruct((tokens, QUERY_HEADS * HEAD_SIZE), bf16),
        in_specs=[smem, smem, hbm, vmem] + [hbm] * 5,
        out_specs=hbm,
        scratch_shapes=[
            pltpu.VMEM((2, tokens, width), bf16),
            pltpu.VMEM((2, 8, 128), jnp.int32),
            pltpu.VMEM((GROUPS, width, 2 * HEAD_SIZE), bf16),
            pltpu.VMEM((2, tokens, width), bf16),
            pltpu.VMEM((2 * slots, width), bf16),
            pltpu.VMEM((n_ctx * slots, 2 * HEAD_SIZE), bf16),
            pltpu.VMEM((n_z, 8, 2 * slots), jnp.float32),
            pltpu.VMEM((2, tokens, 2 * HEAD_SIZE), bf16),
            pltpu.VMEM((2, GROUP, tokens, HEAD_SIZE), bf16),
            pltpu.VMEM((2, 8, n_ctx * slots), jnp.float32),
            pltpu.VMEM((2, tokens, tokens), jnp.float32),
            pltpu.VMEM((2, GROUP, tokens, HEAD_SIZE), bf16),
            dma((PIECES,)),
            dma((STRIPS,)),
            dma((PIECES,)),
            dma((PIECES,)),
            dma((flows, n_z)),
            dma((flows, n_z)),
            dma((flows, n_z)),
            dma((PIECES, n_z)),
            dma((PIECES, n_z)),
            dma((PIECES, 2)),
            dma((PIECES, 2)),
            dma((STRIPS,)),
            dma((STRIPS,)),
            dma((1,)),
            dma((1,)),
            dma((2, n_z)),
            dma((2, n_z)),
            dma((GROUP,)),
            dma((GROUP,)),
            dma((GROUP,)),
        ],
        compiler_params=pltpu.CompilerParams(
            collective_id=0, has_side_effects=True, vmem_limit_bytes=56 * 2**20
        ),
    )(
        hist_len,
        ratio_level,
        hidden_in[0],
        norm_gain,
        w_query,
        w_key,
        value_weight,
        marker_key_weight,
        marker_value_weight,
    )
    return result[None]


def solution(mesh):
    n_dp, n_ctx = mesh.shape["dp"], mesh.shape["ctx"]

    def body(*args):
        tokens, rows = args[0].shape[1], args[2].shape[0]
        if rows % 16 == 0 and tokens == 256 and n_dp == 4 and n_ctx % 2 == 0 and n_ctx > 2:
            return on_device_paired(n_dp, n_ctx, *args)
        return on_device(*args)

    return jax.shard_map(
        body,
        mesh=mesh,
        in_specs=(
            P("dp", "ctx", None),
            P(),
            P(("dp", "ctx"), None),
            P(("dp", "ctx"), None),
            P(("dp", "ctx"), None),
            P(("dp", "ctx"), None),
            P(("dp", "ctx"), None),
            P("dp", "ctx"),
            P("dp"),
        ),
        out_specs=P("dp", "ctx", None),
        check_vma=False,
    )
```

```python
import functools
import math

import jax
import jax.numpy as jnp
from jax import lax
from jax.experimental import pallas as pl
from jax.experimental.pallas import tpu as pltpu
from jax.sharding import PartitionSpec as P

QUERY_HEADS = 14
KEY_VALUE_HEADS = 2
HEAD_SIZE = 128


eps_norm = 1e-06
negative_filler = -1e30


def norm_rows(tokens, norm_gain):
    values = tokens.astype(jnp.float32)
    factor = lax.rsqrt(jnp.mean(values * values, axis=-1, keepdims=True) + eps_norm)
    return (values * factor * norm_gain).astype(jnp.bfloat16)


def window_table(span_level, begin_offset, length, token_rows, marker_slot_count):
    stride = (4 * jnp.power(2, span_level)).astype(jnp.int32)
    live_count = token_rows // stride
    slot_ids = lax.broadcasted_iota(jnp.int32, (marker_slot_count, token_rows), 0)
    pos_ids = lax.broadcasted_iota(jnp.int32, (marker_slot_count, token_rows), 1)
    inside = (
        (pos_ids // stride == slot_ids)
        & (slot_ids < live_count)
        & (begin_offset + pos_ids < length)
    )
    slot_col = jnp.arange(marker_slot_count, dtype=jnp.int32)
    live_slot = (slot_col < live_count) & (begin_offset + slot_col * stride < length)
    return (inside, live_slot)


def pool_rows(inside, normed):
    window_sum = jnp.dot(inside.astype(jnp.bfloat16), normed, preferred_element_type=jnp.float32)
    window_size = jnp.sum(inside.astype(jnp.float32), axis=1)
    return (window_sum / jnp.maximum(window_size, 1.0)[:, None]).astype(jnp.bfloat16)


def raw_attention(query_matrix, key_matrix, value_matrix, begin_offset, length, score_scale):
    token_rows = key_matrix.shape[0]
    scores = (
        jnp.einsum("kgtd,skd->kgts", query_matrix, key_matrix, preferred_element_type=jnp.float32)
        * score_scale
    )
    positions = jnp.arange(token_rows, dtype=jnp.int32)
    visible = (positions[None, :] <= positions[:, None]) & (
        begin_offset + positions[None, :] < length
    )
    scores = jnp.where(visible, scores, negative_filler)
    top_score = jnp.max(scores, axis=-1)
    weights = jnp.where(visible, jnp.exp(scores - top_score[..., None]), 0.0)
    weight_sum = jnp.sum(weights, axis=-1)
    weighted = jnp.einsum(
        "kgts,skd->kgtd",
        weights.astype(jnp.bfloat16),
        value_matrix,
        preferred_element_type=jnp.float32,
    )
    return (top_score, weight_sum, weighted)


def beacon_update(
    carry_state,
    query_matrix,
    limit,
    marker_key_rows,
    marker_value_rows,
    beacon_live,
    marker_slot_count,
    score_scale,
):
    row_total = marker_key_rows.shape[0]
    span_of = jnp.arange(row_total, dtype=jnp.int32) // marker_slot_count
    visible = (beacon_live > 0) & (span_of < limit)

    def compute(state):
        running, weight_sum, weighted = state
        scores = (
            jnp.einsum(
                "kgtd,skd->kgts", query_matrix, marker_key_rows, preferred_element_type=jnp.float32
            )
            * score_scale
        )
        scores = jnp.where(visible, scores, negative_filler)
        new_top = jnp.maximum(running, jnp.max(scores, axis=-1))
        weights = jnp.where(visible, jnp.exp(scores - new_top[..., None]), 0.0)
        added = jnp.einsum(
            "kgts,skd->kgtd",
            weights.astype(jnp.bfloat16),
            marker_value_rows,
            preferred_element_type=jnp.float32,
        )
        return (new_top, jnp.sum(weights, axis=-1), added)

    def unchanged(state):
        return state

    return lax.cond(jnp.any(visible), compute, unchanged, carry_state)


def on_device(
    hidden_in,
    norm_gain,
    w_query,
    w_key,
    value_weight,
    marker_key_weight,
    marker_value_weight,
    ratio_level,
    hist_len,
):
    token_rows = hidden_in.shape[1]
    marker_slot_count = token_rows // 4
    my_span = lax.axis_index("ctx")
    begin_offset = my_span * token_rows
    length = hist_len[0]
    query_group_count = QUERY_HEADS // KEY_VALUE_HEADS
    score_scale = 1.0 / math.sqrt(HEAD_SIZE)
    normed = norm_rows(hidden_in[0], norm_gain)
    inside, live_slot = window_table(
        ratio_level[0, 0], begin_offset, length, token_rows, marker_slot_count
    )
    pooled = pool_rows(inside, normed)
    local_part = (
        lax.all_gather(w_query, "ctx", axis=0, tiled=True),
        lax.all_gather(w_key, "ctx", axis=0, tiled=True),
        lax.all_gather(value_weight, "ctx", axis=0, tiled=True),
        lax.all_gather(marker_key_weight, "ctx", axis=0, tiled=True),
        lax.all_gather(marker_value_weight, "ctx", axis=0, tiled=True),
    )
    segment_list = (
        lax.all_gather(local_part[0], "dp", axis=0, tiled=True),
        lax.all_gather(local_part[1], "dp", axis=0, tiled=True),
        lax.all_gather(local_part[2], "dp", axis=0, tiled=True),
        lax.all_gather(local_part[3], "dp", axis=0, tiled=True),
        lax.all_gather(local_part[4], "dp", axis=0, tiled=True),
    )
    flattened_query = jnp.dot(normed, segment_list[0], preferred_element_type=jnp.float32).astype(
        jnp.bfloat16
    )
    query_matrix = flattened_query.reshape(
        token_rows, KEY_VALUE_HEADS, query_group_count, HEAD_SIZE
    ).transpose(1, 2, 0, 3)
    key_matrix = (
        jnp.dot(normed, segment_list[1], preferred_element_type=jnp.float32)
        .astype(jnp.bfloat16)
        .reshape(token_rows, KEY_VALUE_HEADS, HEAD_SIZE)
    )
    value_matrix = (
        jnp.dot(normed, segment_list[2], preferred_element_type=jnp.float32)
        .astype(jnp.bfloat16)
        .reshape(token_rows, KEY_VALUE_HEADS, HEAD_SIZE)
    )
    marker_key_rows = jnp.dot(pooled, segment_list[3], preferred_element_type=jnp.float32).astype(
        jnp.bfloat16
    )
    marker_value_rows = jnp.dot(pooled, segment_list[4], preferred_element_type=jnp.float32).astype(
        jnp.bfloat16
    )
    raw_top, raw_sum, raw_weighted = raw_attention(
        query_matrix, key_matrix, value_matrix, begin_offset, length, score_scale
    )
    halved_rows = token_rows // 2
    first_q = query_matrix[:, :, :halved_rows]
    second_q = query_matrix[:, :, halved_rows:]
    empty_state = (
        jnp.full((KEY_VALUE_HEADS, query_group_count, halved_rows), negative_filler, jnp.float32),
        jnp.zeros((KEY_VALUE_HEADS, query_group_count, halved_rows), jnp.float32),
        jnp.zeros((KEY_VALUE_HEADS, query_group_count, halved_rows, HEAD_SIZE), jnp.float32),
    )
    segment_list = (
        lax.all_gather(marker_key_rows, "ctx", axis=0, tiled=True),
        lax.all_gather(marker_value_rows, "ctx", axis=0, tiled=True),
        lax.all_gather(live_slot.astype(jnp.bfloat16), "ctx", axis=0, tiled=True),
    )
    segment_keys = segment_list[0].reshape(-1, KEY_VALUE_HEADS, HEAD_SIZE)
    segment_values = segment_list[1].reshape(-1, KEY_VALUE_HEADS, HEAD_SIZE)
    first_state = beacon_update(
        empty_state,
        first_q,
        my_span,
        segment_keys,
        segment_values,
        segment_list[2],
        marker_slot_count,
        score_scale,
    )
    second_state = beacon_update(
        empty_state,
        second_q,
        my_span,
        segment_keys,
        segment_values,
        segment_list[2],
        marker_slot_count,
        score_scale,
    )
    first_state, second_state = (first_state, second_state)
    beacon_top = jnp.concatenate([first_state[0], second_state[0]], axis=2)
    beacon_sum = jnp.concatenate([first_state[1], second_state[1]], axis=2)
    beacon_weighted = jnp.concatenate([first_state[2], second_state[2]], axis=2)
    joint_top = jnp.maximum(raw_top, beacon_top)
    raw_factor = jnp.exp(raw_top - joint_top)
    beacon_factor = jnp.exp(beacon_top - joint_top)
    weight_sum = raw_sum * raw_factor + beacon_sum * beacon_factor
    weighted = raw_weighted * raw_factor[..., None] + beacon_weighted * beacon_factor[..., None]
    result = weighted / jnp.where(weight_sum > 0, weight_sum, 1.0)[..., None]
    result = result.transpose(2, 0, 1, 3).reshape(token_rows, QUERY_HEADS * HEAD_SIZE)
    valid = begin_offset + jnp.arange(token_rows, dtype=jnp.int32) < length
    result = jnp.where(valid[:, None], result, 0.0).astype(jnp.bfloat16)
    return result[None]


GROUP = QUERY_HEADS // KEY_VALUE_HEADS
PIECES = 4 + GROUP
GROUPS = (PIECES + 1) // 2
AHEAD = 5
Y_FIRST = (PIECES - 2, PIECES - 1)
FLOWS = [(p, 0) for p in range(PIECES)] + [(p, 1) for p in Y_FIRST]
STRIPS = 4
MESH = pl.DeviceIdType.MESH


def sublayer_kernel(
    n_dp,
    n_ctx,
    length_ref,
    level_ref,
    hidden_hbm,
    gain_ref,
    wq_ref,
    wk_ref,
    wv_ref,
    mk_ref,
    mv_ref,
    out_ref,
    hidden,
    levels,
    weights_buf,
    normed,
    pooled,
    beacons,
    live_bias,
    kv_buf,
    q_buf,
    span_bias,
    raw_bias,
    made_out,
    own_sem,
    load_sem,
    xs,
    xr,
    zu,
    zd,
    zr,
    ys,
    yr,
    cs,
    cr,
    hs,
    hr,
    ls,
    lr,
    bs,
    br,
    os_,
    or_,
    keep_sem,
):
    tokens = hidden_hbm.shape[0]
    rows = wq_ref.shape[0]
    slots = tokens // 4
    n_z = n_ctx // 2
    pair = 2 * slots
    dp = lax.axis_index("dp")
    ctx = lax.axis_index("ctx")
    z, x = ctx // 2, lax.rem(ctx, 2)
    other_x = 1 - x
    x_peer = (dp, z * 2 + other_x)
    y_dp = lax.rem(dp + n_dp // 2, n_dp)
    y_peer = (y_dp, ctx)
    mate = (dp + 1 - 2 * lax.rem(dp, 2), ctx)
    has_up, has_down = z + 1 < n_z, z > 0
    z_up = (dp, lax.rem(z + 1, n_z) * 2 + x)
    z_down = (dp, lax.rem(z + n_z - 1, n_z) * 2 + x)

    barrier = pltpu.get_barrier_semaphore()

    def greet(peer):
        pl.semaphore_signal(barrier, inc=1, device_id=peer, device_id_type=MESH)

    for peer in (x_peer, y_peer, mate):
        greet(peer)

    @pl.when(has_up)
    def _():
        greet(z_up)

    @pl.when(has_down)
    def _():
        greet(z_down)

    def remote(source, target, send, recv, peer):
        return pltpu.make_async_remote_copy(
            src_ref=source,
            dst_ref=target,
            send_sem=send,
            recv_sem=recv,
            device_id=peer,
            device_id_type=MESH,
        )

    strip = tokens // STRIPS

    def load_copy(i):
        part = pl.ds(i * strip, strip)
        return pltpu.make_async_copy(
            hidden_hbm.at[part, :], hidden.at[0, part, :], load_sem.at[i]
        )

    for i in range(STRIPS):
        load_copy(i).start()

    def piece_source(p, head):
        if p < 4:
            ref = (mk_ref, mv_ref, wk_ref, wv_ref)[p]
            column = head * HEAD_SIZE
        else:
            ref = wq_ref
            column = (head * GROUP + p - 4) * HEAD_SIZE
        return ref.at[:, pl.ds(pl.multiple_of(column, HEAD_SIZE), HEAD_SIZE)]

    def piece_rows(p, start, count):
        return weights_buf.at[
            p // 2,
            pl.ds(pl.multiple_of(start * rows, 16), count * rows),
            pl.ds((p % 2) * HEAD_SIZE, HEAD_SIZE),
        ]

    me = dp * n_ctx + ctx

    def amount(blocks):
        for a in range(1, GROUPS + 1):
            if blocks % (2 * a) == 0 and blocks // (2 * a) <= n_dp * n_ctx:
                return weights_buf.at[0:a, 0 : blocks // (2 * a) * rows, :]
        return weights_buf.at[0, 0 : blocks * rows, 0:HEAD_SIZE]

    def own_copy(p):
        return pltpu.make_async_copy(piece_source(p, x), piece_rows(p, me, 1), own_sem)

    def x_copy(p):
        return remote(piece_source(p, other_x), piece_rows(p, me, 1), xs, xr.at[p], x_peer)

    for p in range(PIECES):
        own_copy(p).start()

    for m in range(1, n_z):

        @pl.when(z < m)
        def _():
            beacons[m * pair : (m + 1) * pair, :] = jnp.zeros(
                (pair, 2 * HEAD_SIZE), jnp.bfloat16
            )
            live_bias[m] = jnp.full((8, pair), negative_filler, jnp.float32)

    levels[x] = jnp.broadcast_to(level_ref[0, 0], (8, 128))
    length = length_ref[0]

    pl.semaphore_wait(
        barrier, 3 + has_up.astype(jnp.int32) + has_down.astype(jnp.int32)
    )

    def z_copy(f, source, step):
        p, column = FLOWS[f]
        block = piece_rows(p, (dp, y_dp)[column] * n_ctx + source * 2, 2)
        sends = zu if step > 0 else zd
        peer = z_up if step > 0 else z_down
        return remote(block, block, sends, zr.at[f, source], peer)

    def y_copy(p, source):
        block = piece_rows(p, dp * n_ctx + source * 2, 2)
        return remote(block, block, ys, yr.at[p], y_peer)

    def c_copy(p, which):
        block = piece_rows(p, (dp, y_dp)[which] * n_ctx, n_ctx)
        return remote(block, block, cs, cr.at[p // 2], mate)

    def begin(p):
        x_copy(p).wait_recv()
        y_copy(p, z).start()

    def launch(f):
        p, column = FLOWS[f]
        if column == 1:
            y_copy(p, z).wait_recv()
        elif p not in Y_FIRST:
            begin(p)

        @pl.when(has_up)
        def _():
            z_copy(f, z, 1).start()

        @pl.when(has_down)
        def _():
            z_copy(f, z, -1).start()

    def relay(f, d):
        p, column = FLOWS[f]
        spread = column == 0 and p not in Y_FIRST

        @pl.when(z - d >= 0)
        def _():
            z_copy(f, z - d, 1).wait_recv()
            if spread:
                y_copy(p, z - d).start()

            @pl.when(has_up)
            def _():
                z_copy(f, z - d, 1).start()

        @pl.when(z + d < n_z)
        def _():
            z_copy(f, z + d, -1).wait_recv()
            if spread:
                y_copy(p, z + d).start()

            @pl.when(has_down)
            def _():
                z_copy(f, z + d, -1).start()

        if d == n_z - 1:
            c_copy(p, column).start()

    def tick(t):
        for d in range(1, n_z):
            f = t - d + 1
            if 0 <= f < len(FLOWS):
                relay(f, d)
        if t + AHEAD < len(FLOWS):
            launch(t + AHEAD)

    def y_arrived(p):
        if p not in Y_FIRST:
            block = piece_rows(p, y_dp * n_ctx, n_ctx)
            remote(block, block, ys, yr.at[p], y_peer).wait_recv()
            c_copy(p, 1).start()

    def arrived(g):
        last = HEAD_SIZE * (1 + min(1, PIECES - 1 - 2 * g))
        block = weights_buf.at[g, 0 : 2 * n_ctx * rows, 0:last]
        remote(block, block, cs, cr.at[g], mate).wait_recv()

    def hidden_copy(i):
        part = pl.ds(i * strip, strip)
        return remote(
            hidden_hbm.at[part, :], hidden.at[1, part, :], hs, hr.at[i], x_peer
        )

    level_copy = remote(levels.at[x], levels.at[x], ls, lr, x_peer)

    def beacon_rows(first, count):
        return beacons.at[pl.ds(pl.multiple_of(first * slots, slots), count * slots), :]

    def send_up(source, kind, level):
        for d in range(1, n_z):

            @pl.when(z + d < n_z)
            def _():
                peer = (dp, lax.rem(z + d, n_z) * 2 + x)
                remote(source, source, bs.at[kind], br.at[kind, level], peer).start()

    def head_columns(head, j):
        return pl.ds(pl.multiple_of((head * GROUP + j) * HEAD_SIZE, HEAD_SIZE), HEAD_SIZE)

    def out_copy(j):
        return remote(
            made_out.at[1, j], out_ref.at[:, head_columns(x, j)], os_, or_, x_peer
        )

    def keep_copy(j):
        return pltpu.make_async_copy(
            made_out.at[0, j], out_ref.at[:, head_columns(x, j)], keep_sem
        )

    def half(head):
        width = GROUP * HEAD_SIZE
        return out_ref.at[:, pl.ds(pl.multiple_of(head * width, HEAD_SIZE), width)]

    for p in range(PIECES):
        x_copy(p).start()
    level_copy.start()
    for i in range(STRIPS):
        hidden_copy(i).start()

    gain = gain_ref[...][None, :]

    def norm_strip(i, which, slot):
        def body(k, carry):
            part = pl.ds(pl.multiple_of(i * strip + k * 16, 16), 16)
            values = hidden[which, part, :].astype(jnp.float32)
            factor = lax.rsqrt(jnp.mean(values * values, axis=-1, keepdims=True) + eps_norm)
            normed[slot, part, :] = (values * factor * gain).astype(jnp.bfloat16)
            return carry

        lax.fori_loop(0, strip // 16, body, 0)

    def norm_own(i):
        load_copy(i).wait()
        norm_strip(i, 0, x)

    def norm_other(i):
        hidden_copy(i).wait_recv()
        norm_strip(i, 1, other_x)

    lane = lax.broadcasted_iota(jnp.int32, (1, pair), 1)
    slot_id = lax.rem(lane, slots)
    sub = lane // slots

    def stride_of(level):
        return jnp.where(
            level == 0, 4, jnp.where(level == 1, 8, jnp.where(level == 2, 16, 32))
        )

    def own_live():
        level = jnp.where(sub == 0, levels[0, 0:1, :], levels[1, 0:1, :])
        stride = stride_of(level)
        owner = 2 * z + sub
        live = (slot_id * stride < tokens) & (owner * tokens + slot_id * stride < length)
        live_bias[z] = jnp.broadcast_to(jnp.where(live, 0.0, negative_filler), (8, pair))
        send_up(live_bias.at[z], 1, z)

    def mask_far():
        for s in range(2):
            for m in range(n_z):
                seen = (2 * m + sub) < (2 * z + s)
                span_bias[s, :, m * pair : (m + 1) * pair] = jnp.where(
                    seen, live_bias[m], negative_filler
                )

    def mask_near():
        for s in range(2):
            row_id = lax.broadcasted_iota(jnp.int32, (tokens, tokens), 0)
            col_id = lax.broadcasted_iota(jnp.int32, (tokens, tokens), 1)
            seen = (col_id <= row_id) & ((z * 2 + s) * tokens + col_id < length)
            raw_bias[s] = jnp.where(seen, 0.0, negative_filler)

    def pool(s):
        span = z * 2 + s
        level = jnp.broadcast_to(levels[s, 0:1, :], (slots, 128))
        stride = stride_of(level)
        slot = lax.broadcasted_iota(jnp.int32, (slots, 128), 0)
        parts = []
        for b in range(tokens // 128):
            pos = lax.broadcasted_iota(jnp.int32, (slots, 128), 1) + b * 128
            inside = (
                (pos >= slot * stride)
                & (pos < (slot + 1) * stride)
                & (span * tokens + pos < length)
            )
            parts.append(jnp.where(inside, 1.0, 0.0))
        inside = jnp.concatenate(parts, axis=1)
        scale = 1.0 / jnp.maximum(jnp.sum(inside, axis=1, keepdims=True), 1.0)
        table = inside.astype(jnp.bfloat16)
        width = normed.shape[2] // 4

        def body(i, carry):
            cols = pl.ds(pl.multiple_of(i * width, 128), width)
            total = jnp.dot(table, normed[s, :, cols], preferred_element_type=jnp.float32)
            pooled[pl.ds(pl.multiple_of(s * slots, slots), slots), cols] = (
                total * scale
            ).astype(jnp.bfloat16)
            return carry

        lax.fori_loop(0, 4, body, 0)

    def project_kv(s):
        kv_buf[s] = jnp.dot(
            normed[s], weights_buf[1], preferred_element_type=jnp.float32
        ).astype(jnp.bfloat16)

    def project_query(s, g):
        result = jnp.dot(
            normed[s], weights_buf[g], preferred_element_type=jnp.float32
        ).astype(jnp.bfloat16)
        q_buf[s, 2 * (g - 2)] = result[:, :HEAD_SIZE]
        q_buf[s, 2 * (g - 2) + 1] = result[:, HEAD_SIZE:]

    def project_last(s):
        q_buf[s, GROUP - 1] = jnp.dot(
            normed[s], weights_buf[GROUPS - 1, :, :HEAD_SIZE], preferred_element_type=jnp.float32
        ).astype(jnp.bfloat16)

    def make_beacons(s):
        part = pl.ds(pl.multiple_of(s * slots, slots), slots)
        made = jnp.dot(pooled[part, :], weights_buf[0], preferred_element_type=jnp.float32)
        block = beacon_rows(z * 2 + s, 1)
        block[...] = made.astype(jnp.bfloat16)
        send_up(block, 0, z)

    def await_beacons():
        for m in range(n_z - 1):

            @pl.when(m < z)
            def _():
                block = beacon_rows(2 * m, 2)
                remote(block, block, bs.at[0], br.at[0, m], x_peer).wait_recv()
                bias = live_bias.at[m]
                remote(bias, bias, bs.at[1], br.at[1, m], x_peer).wait_recv()

        mask_far()

    factor = math.log2(math.e) / math.sqrt(HEAD_SIZE)
    contract = (((1,), (1,)), ((), ()))

    def attend(s, j, which, width):
        query = q_buf[s, j]
        far = lax.dot_general(
            query, beacons[:width, :HEAD_SIZE], contract, preferred_element_type=jnp.float32
        )
        near = lax.dot_general(
            query, kv_buf[s, :, :HEAD_SIZE], contract, preferred_element_type=jnp.float32
        )
        far = far * factor + span_bias[s, 0:1, :width]
        near = near * factor + raw_bias[s]
        top = jnp.maximum(
            jnp.max(far, axis=1, keepdims=True), jnp.max(near, axis=1, keepdims=True)
        )
        far = jnp.exp2(far - top)
        near = jnp.exp2(near - top)
        total = jnp.sum(far, axis=1, keepdims=True) + jnp.sum(near, axis=1, keepdims=True)
        mixed = jnp.dot(
            far.astype(jnp.bfloat16),
            beacons[:width, HEAD_SIZE:],
            preferred_element_type=jnp.float32,
        ) + jnp.dot(
            near.astype(jnp.bfloat16),
            kv_buf[s, :, HEAD_SIZE:],
            preferred_element_type=jnp.float32,
        )
        position = (z * 2 + s) * tokens + lax.broadcasted_iota(jnp.int32, (tokens, 1), 0)
        scale = jnp.where(position < length, 1.0 / total, 0.0)
        made_out[which, j] = (mixed * scale).astype(jnp.bfloat16)

    def heads(first, last):
        def step(j, carry):
            for which, s in ((1, other_x), (0, x)):

                @pl.when(z == 0)
                def _():
                    attend(s, j, which, pair)

                @pl.when(z > 0)
                def _():
                    attend(s, j, which, n_z * pair)

                (keep_copy, out_copy)[which](j).start()
            return carry

        lax.fori_loop(first, last, step, 0)

    pltpu.make_async_copy(amount(PIECES), amount(PIECES), own_sem).wait()
    for f in range(AHEAD):
        launch(f)
    for i in range(STRIPS):
        norm_own(i)
    for p in Y_FIRST:
        begin(p)
    tick(0)
    pool(x)
    mask_near()
    tick(1)
    tick(2)
    norm_other(0)
    tick(3)
    y_arrived(0)
    tick(4)
    level_copy.wait_recv()
    own_live()
    y_arrived(1)
    tick(5)
    y_arrived(2)
    norm_other(1)
    tick(6)
    y_arrived(3)
    tick(7)
    y_arrived(4)
    arrived(1)
    project_kv(x)
    tick(8)
    y_arrived(5)
    norm_other(2)
    arrived(2)
    project_query(x, 2)
    tick(9)
    y_arrived(6)
    arrived(0)
    make_beacons(x)
    tick(10)
    y_arrived(7)
    norm_other(3)
    pool(other_x)
    make_beacons(other_x)
    project_kv(other_x)
    tick(11)
    y_arrived(8)
    arrived(3)
    project_query(x, 3)
    project_query(other_x, 2)
    tick(12)
    y_arrived(9)
    await_beacons()
    heads(0, 2)
    tick(13)
    y_arrived(10)
    project_query(other_x, 3)
    heads(2, 4)
    tick(14)
    arrived(4)
    project_query(x, 4)
    project_query(other_x, 4)
    heads(4, 6)
    arrived(5)
    project_last(x)
    project_last(other_x)
    heads(6, 7)
    pltpu.make_async_copy(half(x), half(x), keep_sem).wait()
    remote(half(other_x), half(other_x), os_, or_, x_peer).wait()
    remote(amount(PIECES), amount(PIECES), xs, xr.at[0], x_peer).wait_send()
    every = amount((PIECES - len(Y_FIRST)) * 2 * n_z + 2 * len(Y_FIRST))
    remote(every, every, ys, yr.at[0], y_peer).wait_send()
    every = amount(PIECES * 2 * n_ctx)
    remote(every, every, cs, cr.at[0], mate).wait_send()
    for m in range(n_z):

        @pl.when(has_up & (z == m))
        def _():
            every = amount(len(FLOWS) * 2 * (m + 1))
            remote(every, every, zu, zr.at[0, 0], z_up).wait_send()
            every = beacons.at[0 : (n_z - 1 - m) * pair, :]
            remote(every, every, bs.at[0], br.at[0, 0], z_up).wait_send()
            every = live_bias.at[0 : n_z - 1 - m]
            remote(every, every, bs.at[1], br.at[1, 0], z_up).wait_send()

        @pl.when(has_down & (z == m))
        def _():
            every = amount(len(FLOWS) * 2 * (n_z - m))
            remote(every, every, zd, zr.at[0, 0], z_down).wait_send()

    remote(hidden_hbm, hidden.at[1], hs, hr.at[0], x_peer).wait_send()
    level_copy.wait_send()


def on_device_paired(
    n_dp,
    n_ctx,
    hidden_in,
    norm_gain,
    w_query,
    w_key,
    value_weight,
    marker_key_weight,
    marker_value_weight,
    ratio_level,
    hist_len,
):
    tokens, width = hidden_in.shape[1:]
    slots = tokens // 4
    n_z = n_ctx // 2
    flows = len(FLOWS)
    dma = pltpu.SemaphoreType.DMA
    vmem = pl.BlockSpec(memory_space=pltpu.VMEM)
    smem = pl.BlockSpec(memory_space=pltpu.SMEM)
    hbm = pl.BlockSpec(memory_space=pl.ANY)
    bf16 = jnp.bfloat16
    result = pl.pallas_call(
        functools.partial(sublayer_kernel, n_dp, n_ctx),
        out_shape=jax.ShapeDtypeStruct((tokens, QUERY_HEADS * HEAD_SIZE), bf16),
        in_specs=[smem, smem, hbm, vmem] + [hbm] * 5,
        out_specs=hbm,
        scratch_shapes=[
            pltpu.VMEM((2, tokens, width), bf16),
            pltpu.VMEM((2, 8, 128), jnp.int32),
            pltpu.VMEM((GROUPS, width, 2 * HEAD_SIZE), bf16),
            pltpu.VMEM((2, tokens, width), bf16),
            pltpu.VMEM((2 * slots, width), bf16),
            pltpu.VMEM((n_ctx * slots, 2 * HEAD_SIZE), bf16),
            pltpu.VMEM((n_z, 8, 2 * slots), jnp.float32),
            pltpu.VMEM((2, tokens, 2 * HEAD_SIZE), bf16),
            pltpu.VMEM((2, GROUP, tokens, HEAD_SIZE), bf16),
            pltpu.VMEM((2, 8, n_ctx * slots), jnp.float32),
            pltpu.VMEM((2, tokens, tokens), jnp.float32),
            pltpu.VMEM((2, GROUP, tokens, HEAD_SIZE), bf16),
            dma,
            dma((STRIPS,)),
            dma,
            dma((PIECES,)),
            dma,
            dma,
            dma((flows, n_z)),
            dma,
            dma((PIECES,)),
            dma,
            dma((GROUPS,)),
            dma,
            dma((STRIPS,)),
            dma,
            dma,
            dma((2,)),
            dma((2, n_z)),
            dma,
            dma,
            dma,
        ],
        compiler_params=pltpu.CompilerParams(
            collective_id=0, has_side_effects=True, vmem_limit_bytes=56 * 2**20
        ),
    )(
        hist_len,
        ratio_level,
        hidden_in[0],
        norm_gain,
        w_query,
        w_key,
        value_weight,
        marker_key_weight,
        marker_value_weight,
    )
    return result[None]


def solution(mesh):
    n_dp, n_ctx = mesh.shape["dp"], mesh.shape["ctx"]

    def body(*args):
        tokens, rows = args[0].shape[1], args[2].shape[0]
        if rows % 16 == 0 and tokens == 256 and n_dp == 4 and n_ctx % 2 == 0 and n_ctx > 2:
            return on_device_paired(n_dp, n_ctx, *args)
        return on_device(*args)

    return jax.shard_map(
        body,
        mesh=mesh,
        in_specs=(
            P("dp", "ctx", None),
            P(),
            P(("dp", "ctx"), None),
            P(("dp", "ctx"), None),
            P(("dp", "ctx"), None),
            P(("dp", "ctx"), None),
            P(("dp", "ctx"), None),
            P("dp", "ctx"),
            P("dp"),
        ),
        out_specs=P("dp", "ctx", None),
        check_vma=False,
    )
```

```python
import functools
import math

import jax
import jax.numpy as jnp
from jax import lax
from jax.experimental import pallas as pl
from jax.experimental.pallas import tpu as pltpu
from jax.sharding import PartitionSpec as P

QUERY_HEADS = 14
KEY_VALUE_HEADS = 2
HEAD_SIZE = 128


eps_norm = 1e-06
negative_filler = -1e30


def norm_rows(tokens, norm_gain):
    values = tokens.astype(jnp.float32)
    factor = lax.rsqrt(jnp.mean(values * values, axis=-1, keepdims=True) + eps_norm)
    return (values * factor * norm_gain).astype(jnp.bfloat16)


def window_table(span_level, begin_offset, length, token_rows, marker_slot_count):
    stride = (4 * jnp.power(2, span_level)).astype(jnp.int32)
    live_count = token_rows // stride
    slot_ids = lax.broadcasted_iota(jnp.int32, (marker_slot_count, token_rows), 0)
    pos_ids = lax.broadcasted_iota(jnp.int32, (marker_slot_count, token_rows), 1)
    inside = (
        (pos_ids // stride == slot_ids)
        & (slot_ids < live_count)
        & (begin_offset + pos_ids < length)
    )
    slot_col = jnp.arange(marker_slot_count, dtype=jnp.int32)
    live_slot = (slot_col < live_count) & (begin_offset + slot_col * stride < length)
    return (inside, live_slot)


def pool_rows(inside, normed):
    window_sum = jnp.dot(inside.astype(jnp.bfloat16), normed, preferred_element_type=jnp.float32)
    window_size = jnp.sum(inside.astype(jnp.float32), axis=1)
    return (window_sum / jnp.maximum(window_size, 1.0)[:, None]).astype(jnp.bfloat16)


def raw_attention(query_matrix, key_matrix, value_matrix, begin_offset, length, score_scale):
    token_rows = key_matrix.shape[0]
    scores = (
        jnp.einsum("kgtd,skd->kgts", query_matrix, key_matrix, preferred_element_type=jnp.float32)
        * score_scale
    )
    positions = jnp.arange(token_rows, dtype=jnp.int32)
    visible = (positions[None, :] <= positions[:, None]) & (
        begin_offset + positions[None, :] < length
    )
    scores = jnp.where(visible, scores, negative_filler)
    top_score = jnp.max(scores, axis=-1)
    weights = jnp.where(visible, jnp.exp(scores - top_score[..., None]), 0.0)
    weight_sum = jnp.sum(weights, axis=-1)
    weighted = jnp.einsum(
        "kgts,skd->kgtd",
        weights.astype(jnp.bfloat16),
        value_matrix,
        preferred_element_type=jnp.float32,
    )
    return (top_score, weight_sum, weighted)


def beacon_update(
    carry_state,
    query_matrix,
    limit,
    marker_key_rows,
    marker_value_rows,
    beacon_live,
    marker_slot_count,
    score_scale,
):
    row_total = marker_key_rows.shape[0]
    span_of = jnp.arange(row_total, dtype=jnp.int32) // marker_slot_count
    visible = (beacon_live > 0) & (span_of < limit)

    def compute(state):
        running, weight_sum, weighted = state
        scores = (
            jnp.einsum(
                "kgtd,skd->kgts", query_matrix, marker_key_rows, preferred_element_type=jnp.float32
            )
            * score_scale
        )
        scores = jnp.where(visible, scores, negative_filler)
        new_top = jnp.maximum(running, jnp.max(scores, axis=-1))
        weights = jnp.where(visible, jnp.exp(scores - new_top[..., None]), 0.0)
        added = jnp.einsum(
            "kgts,skd->kgtd",
            weights.astype(jnp.bfloat16),
            marker_value_rows,
            preferred_element_type=jnp.float32,
        )
        return (new_top, jnp.sum(weights, axis=-1), added)

    def unchanged(state):
        return state

    return lax.cond(jnp.any(visible), compute, unchanged, carry_state)


def on_device(
    hidden_in,
    norm_gain,
    w_query,
    w_key,
    value_weight,
    marker_key_weight,
    marker_value_weight,
    ratio_level,
    hist_len,
):
    token_rows = hidden_in.shape[1]
    marker_slot_count = token_rows // 4
    my_span = lax.axis_index("ctx")
    begin_offset = my_span * token_rows
    length = hist_len[0]
    query_group_count = QUERY_HEADS // KEY_VALUE_HEADS
    score_scale = 1.0 / math.sqrt(HEAD_SIZE)
    normed = norm_rows(hidden_in[0], norm_gain)
    inside, live_slot = window_table(
        ratio_level[0, 0], begin_offset, length, token_rows, marker_slot_count
    )
    pooled = pool_rows(inside, normed)
    local_part = (
        lax.all_gather(w_query, "ctx", axis=0, tiled=True),
        lax.all_gather(w_key, "ctx", axis=0, tiled=True),
        lax.all_gather(value_weight, "ctx", axis=0, tiled=True),
        lax.all_gather(marker_key_weight, "ctx", axis=0, tiled=True),
        lax.all_gather(marker_value_weight, "ctx", axis=0, tiled=True),
    )
    segment_list = (
        lax.all_gather(local_part[0], "dp", axis=0, tiled=True),
        lax.all_gather(local_part[1], "dp", axis=0, tiled=True),
        lax.all_gather(local_part[2], "dp", axis=0, tiled=True),
        lax.all_gather(local_part[3], "dp", axis=0, tiled=True),
        lax.all_gather(local_part[4], "dp", axis=0, tiled=True),
    )
    flattened_query = jnp.dot(normed, segment_list[0], preferred_element_type=jnp.float32).astype(
        jnp.bfloat16
    )
    query_matrix = flattened_query.reshape(
        token_rows, KEY_VALUE_HEADS, query_group_count, HEAD_SIZE
    ).transpose(1, 2, 0, 3)
    key_matrix = (
        jnp.dot(normed, segment_list[1], preferred_element_type=jnp.float32)
        .astype(jnp.bfloat16)
        .reshape(token_rows, KEY_VALUE_HEADS, HEAD_SIZE)
    )
    value_matrix = (
        jnp.dot(normed, segment_list[2], preferred_element_type=jnp.float32)
        .astype(jnp.bfloat16)
        .reshape(token_rows, KEY_VALUE_HEADS, HEAD_SIZE)
    )
    marker_key_rows = jnp.dot(pooled, segment_list[3], preferred_element_type=jnp.float32).astype(
        jnp.bfloat16
    )
    marker_value_rows = jnp.dot(pooled, segment_list[4], preferred_element_type=jnp.float32).astype(
        jnp.bfloat16
    )
    raw_top, raw_sum, raw_weighted = raw_attention(
        query_matrix, key_matrix, value_matrix, begin_offset, length, score_scale
    )
    halved_rows = token_rows // 2
    first_q = query_matrix[:, :, :halved_rows]
    second_q = query_matrix[:, :, halved_rows:]
    empty_state = (
        jnp.full((KEY_VALUE_HEADS, query_group_count, halved_rows), negative_filler, jnp.float32),
        jnp.zeros((KEY_VALUE_HEADS, query_group_count, halved_rows), jnp.float32),
        jnp.zeros((KEY_VALUE_HEADS, query_group_count, halved_rows, HEAD_SIZE), jnp.float32),
    )
    segment_list = (
        lax.all_gather(marker_key_rows, "ctx", axis=0, tiled=True),
        lax.all_gather(marker_value_rows, "ctx", axis=0, tiled=True),
        lax.all_gather(live_slot.astype(jnp.bfloat16), "ctx", axis=0, tiled=True),
    )
    segment_keys = segment_list[0].reshape(-1, KEY_VALUE_HEADS, HEAD_SIZE)
    segment_values = segment_list[1].reshape(-1, KEY_VALUE_HEADS, HEAD_SIZE)
    first_state = beacon_update(
        empty_state,
        first_q,
        my_span,
        segment_keys,
        segment_values,
        segment_list[2],
        marker_slot_count,
        score_scale,
    )
    second_state = beacon_update(
        empty_state,
        second_q,
        my_span,
        segment_keys,
        segment_values,
        segment_list[2],
        marker_slot_count,
        score_scale,
    )
    first_state, second_state = (first_state, second_state)
    beacon_top = jnp.concatenate([first_state[0], second_state[0]], axis=2)
    beacon_sum = jnp.concatenate([first_state[1], second_state[1]], axis=2)
    beacon_weighted = jnp.concatenate([first_state[2], second_state[2]], axis=2)
    joint_top = jnp.maximum(raw_top, beacon_top)
    raw_factor = jnp.exp(raw_top - joint_top)
    beacon_factor = jnp.exp(beacon_top - joint_top)
    weight_sum = raw_sum * raw_factor + beacon_sum * beacon_factor
    weighted = raw_weighted * raw_factor[..., None] + beacon_weighted * beacon_factor[..., None]
    result = weighted / jnp.where(weight_sum > 0, weight_sum, 1.0)[..., None]
    result = result.transpose(2, 0, 1, 3).reshape(token_rows, QUERY_HEADS * HEAD_SIZE)
    valid = begin_offset + jnp.arange(token_rows, dtype=jnp.int32) < length
    result = jnp.where(valid[:, None], result, 0.0).astype(jnp.bfloat16)
    return result[None]


GROUP = QUERY_HEADS // KEY_VALUE_HEADS
PIECES = 4 + GROUP
GROUPS = (PIECES + 1) // 2
AHEAD = 5
Y_FIRST = (PIECES - 2, PIECES - 1)
FLOWS = [(p, 0) for p in range(PIECES)] + [(p, 1) for p in Y_FIRST]
STRIPS = 4
MESH = pl.DeviceIdType.MESH


def sublayer_kernel(
    n_dp,
    n_ctx,
    length_ref,
    level_ref,
    hidden_hbm,
    gain_ref,
    wq_ref,
    wk_ref,
    wv_ref,
    mk_ref,
    mv_ref,
    out_ref,
    hidden,
    levels,
    weights_buf,
    normed,
    pooled,
    beacons,
    live_bias,
    kv_buf,
    q_buf,
    span_bias,
    raw_bias,
    made_out,
    own_sem,
    load_sem,
    xs,
    xr,
    zu,
    zd,
    zr,
    ys,
    yr,
    cs,
    cr,
    hs,
    hr,
    ls,
    lr,
    bs,
    br,
    os_,
    or_,
    keep_sem,
):
    tokens = hidden_hbm.shape[0]
    rows = wq_ref.shape[0]
    slots = tokens // 4
    n_z = n_ctx // 2
    pair = 2 * slots
    dp = lax.axis_index("dp")
    ctx = lax.axis_index("ctx")
    z, x = ctx // 2, lax.rem(ctx, 2)
    other_x = 1 - x
    x_peer = (dp, z * 2 + other_x)
    y_dp = lax.rem(dp + n_dp // 2, n_dp)
    y_peer = (y_dp, ctx)
    mate = (dp + 1 - 2 * lax.rem(dp, 2), ctx)
    has_up, has_down = z + 1 < n_z, z > 0
    z_up = (dp, lax.rem(z + 1, n_z) * 2 + x)
    z_down = (dp, lax.rem(z + n_z - 1, n_z) * 2 + x)

    barrier = pltpu.get_barrier_semaphore()

    def greet(peer):
        pl.semaphore_signal(barrier, inc=1, device_id=peer, device_id_type=MESH)

    for peer in (x_peer, y_peer, mate):
        greet(peer)

    @pl.when(has_up)
    def _():
        greet(z_up)

    @pl.when(has_down)
    def _():
        greet(z_down)

    def remote(source, target, send, recv, peer):
        return pltpu.make_async_remote_copy(
            src_ref=source,
            dst_ref=target,
            send_sem=send,
            recv_sem=recv,
            device_id=peer,
            device_id_type=MESH,
        )

    strip = tokens // STRIPS

    def load_copy(i):
        part = pl.ds(i * strip, strip)
        return pltpu.make_async_copy(
            hidden_hbm.at[part, :], hidden.at[0, part, :], load_sem.at[i]
        )

    for i in range(STRIPS):
        load_copy(i).start()

    def piece_source(p, head):
        if p < 4:
            ref = (mk_ref, mv_ref, wk_ref, wv_ref)[p]
            column = head * HEAD_SIZE
        else:
            ref = wq_ref
            column = (head * GROUP + p - 4) * HEAD_SIZE
        return ref.at[:, pl.ds(pl.multiple_of(column, HEAD_SIZE), HEAD_SIZE)]

    def piece_rows(p, start, count):
        return weights_buf.at[
            p // 2,
            pl.ds(pl.multiple_of(start * rows, 16), count * rows),
            pl.ds((p % 2) * HEAD_SIZE, HEAD_SIZE),
        ]

    me = dp * n_ctx + ctx

    def amount(blocks):
        for a in range(1, GROUPS + 1):
            if blocks % (2 * a) == 0 and blocks // (2 * a) <= n_dp * n_ctx:
                return weights_buf.at[0:a, 0 : blocks // (2 * a) * rows, :]
        return weights_buf.at[0, 0 : blocks * rows, 0:HEAD_SIZE]

    def own_copy(p):
        return pltpu.make_async_copy(piece_source(p, x), piece_rows(p, me, 1), own_sem)

    def x_copy(p):
        return remote(piece_source(p, other_x), piece_rows(p, me, 1), xs, xr.at[p], x_peer)

    for p in range(PIECES):
        own_copy(p).start()

    for m in range(1, n_z):

        @pl.when(z < m)
        def _():
            beacons[m * pair : (m + 1) * pair, :] = jnp.zeros(
                (pair, 2 * HEAD_SIZE), jnp.bfloat16
            )
            live_bias[m] = jnp.full((8, pair), negative_filler, jnp.float32)

    levels[x] = jnp.broadcast_to(level_ref[0, 0], (8, 128))
    length = length_ref[0]

    pl.semaphore_wait(
        barrier, 3 + has_up.astype(jnp.int32) + has_down.astype(jnp.int32)
    )

    def z_copy(f, source, step):
        p, column = FLOWS[f]
        block = piece_rows(p, (dp, y_dp)[column] * n_ctx + source * 2, 2)
        sends = zu if step > 0 else zd
        peer = z_up if step > 0 else z_down
        return remote(block, block, sends, zr.at[f, source], peer)

    def y_copy(p, source):
        block = piece_rows(p, dp * n_ctx + source * 2, 2)
        return remote(block, block, ys, yr.at[p], y_peer)

    def c_copy(p, which):
        block = piece_rows(p, (dp, y_dp)[which] * n_ctx, n_ctx)
        return remote(block, block, cs, cr.at[p // 2], mate)

    def begin(p):
        x_copy(p).wait_recv()
        y_copy(p, z).start()

    def launch(f):
        p, column = FLOWS[f]
        if column == 1:
            y_copy(p, z).wait_recv()
        elif p not in Y_FIRST:
            begin(p)

        @pl.when(has_up)
        def _():
            z_copy(f, z, 1).start()

        @pl.when(has_down)
        def _():
            z_copy(f, z, -1).start()

    def relay(f, d):
        p, column = FLOWS[f]
        spread = column == 0 and p not in Y_FIRST

        @pl.when(z - d >= 0)
        def _():
            z_copy(f, z - d, 1).wait_recv()
            if spread:
                y_copy(p, z - d).start()

            @pl.when(has_up)
            def _():
                z_copy(f, z - d, 1).start()

        @pl.when(z + d < n_z)
        def _():
            z_copy(f, z + d, -1).wait_recv()
            if spread:
                y_copy(p, z + d).start()

            @pl.when(has_down)
            def _():
                z_copy(f, z + d, -1).start()

        if d == n_z - 1:
            c_copy(p, column).start()

    def tick(t):
        for d in range(1, n_z):
            f = t - d + 1
            if 0 <= f < len(FLOWS):
                relay(f, d)
        if t + AHEAD < len(FLOWS):
            launch(t + AHEAD)

    def y_arrived(p):
        if p not in Y_FIRST:
            block = piece_rows(p, y_dp * n_ctx, n_ctx)
            remote(block, block, ys, yr.at[p], y_peer).wait_recv()
            c_copy(p, 1).start()

    def arrived(g):
        last = HEAD_SIZE * (1 + min(1, PIECES - 1 - 2 * g))
        block = weights_buf.at[g, 0 : 2 * n_ctx * rows, 0:last]
        remote(block, block, cs, cr.at[g], mate).wait_recv()

    def hidden_copy(i):
        part = pl.ds(i * strip, strip)
        return remote(
            hidden_hbm.at[part, :], hidden.at[1, part, :], hs, hr.at[i], x_peer
        )

    level_copy = remote(levels.at[x], levels.at[x], ls, lr, x_peer)

    def beacon_rows(first, count):
        return beacons.at[pl.ds(pl.multiple_of(first * slots, slots), count * slots), :]

    def send_up(source, kind, level):
        for d in range(1, n_z):

            @pl.when(z + d < n_z)
            def _():
                peer = (dp, lax.rem(z + d, n_z) * 2 + x)
                remote(source, source, bs.at[kind], br.at[kind, level], peer).start()

    def head_columns(head, j):
        return pl.ds(pl.multiple_of((head * GROUP + j) * HEAD_SIZE, HEAD_SIZE), HEAD_SIZE)

    def out_copy(j):
        return remote(
            made_out.at[1, j], out_ref.at[:, head_columns(x, j)], os_, or_, x_peer
        )

    def keep_copy(j):
        return pltpu.make_async_copy(
            made_out.at[0, j], out_ref.at[:, head_columns(x, j)], keep_sem
        )

    def half(head):
        width = GROUP * HEAD_SIZE
        return out_ref.at[:, pl.ds(pl.multiple_of(head * width, HEAD_SIZE), width)]

    for p in range(PIECES):
        x_copy(p).start()
    level_copy.start()
    for i in range(STRIPS):
        hidden_copy(i).start()

    gain = gain_ref[...][None, :]

    def norm_strip(i, which, slot):
        def body(k, carry):
            part = pl.ds(pl.multiple_of(i * strip + k * 16, 16), 16)
            values = hidden[which, part, :].astype(jnp.float32)
            factor = lax.rsqrt(jnp.mean(values * values, axis=-1, keepdims=True) + eps_norm)
            normed[slot, part, :] = (values * factor * gain).astype(jnp.bfloat16)
            return carry

        lax.fori_loop(0, strip // 16, body, 0)

    def norm_own(i):
        load_copy(i).wait()
        norm_strip(i, 0, x)

    def norm_other(i):
        hidden_copy(i).wait_recv()
        norm_strip(i, 1, other_x)

    lane = lax.broadcasted_iota(jnp.int32, (1, pair), 1)
    slot_id = lax.rem(lane, slots)
    sub = lane // slots

    def stride_of(level):
        return jnp.where(
            level == 0, 4, jnp.where(level == 1, 8, jnp.where(level == 2, 16, 32))
        )

    def own_live():
        level = jnp.where(sub == 0, levels[0, 0:1, :], levels[1, 0:1, :])
        stride = stride_of(level)
        owner = 2 * z + sub
        live = (slot_id * stride < tokens) & (owner * tokens + slot_id * stride < length)
        live_bias[z] = jnp.broadcast_to(jnp.where(live, 0.0, negative_filler), (8, pair))
        send_up(live_bias.at[z], 1, z)

    def mask_far():
        for s in range(2):
            for m in range(n_z):
                seen = (2 * m + sub) < (2 * z + s)
                span_bias[s, :, m * pair : (m + 1) * pair] = jnp.where(
                    seen, live_bias[m], negative_filler
                )

    def mask_near():
        for s in range(2):
            row_id = lax.broadcasted_iota(jnp.int32, (tokens, tokens), 0)
            col_id = lax.broadcasted_iota(jnp.int32, (tokens, tokens), 1)
            seen = (col_id <= row_id) & ((z * 2 + s) * tokens + col_id < length)
            raw_bias[s] = jnp.where(seen, 0.0, negative_filler)

    def pool(s):
        span = z * 2 + s
        level = jnp.broadcast_to(levels[s, 0:1, :], (slots, 128))
        stride = stride_of(level)
        slot = lax.broadcasted_iota(jnp.int32, (slots, 128), 0)
        parts = []
        for b in range(tokens // 128):
            pos = lax.broadcasted_iota(jnp.int32, (slots, 128), 1) + b * 128
            inside = (
                (pos >= slot * stride)
                & (pos < (slot + 1) * stride)
                & (span * tokens + pos < length)
            )
            parts.append(jnp.where(inside, 1.0, 0.0))
        inside = jnp.concatenate(parts, axis=1)
        scale = 1.0 / jnp.maximum(jnp.sum(inside, axis=1, keepdims=True), 1.0)
        table = inside.astype(jnp.bfloat16)
        width = normed.shape[2] // 4

        def body(i, carry):
            cols = pl.ds(pl.multiple_of(i * width, 128), width)
            total = jnp.dot(table, normed[s, :, cols], preferred_element_type=jnp.float32)
            pooled[pl.ds(pl.multiple_of(s * slots, slots), slots), cols] = (
                total * scale
            ).astype(jnp.bfloat16)
            return carry

        lax.fori_loop(0, 4, body, 0)

    def project_kv(s):
        kv_buf[s] = jnp.dot(
            normed[s], weights_buf[1], preferred_element_type=jnp.float32
        ).astype(jnp.bfloat16)

    def project_query(s, g):
        result = jnp.dot(
            normed[s], weights_buf[g], preferred_element_type=jnp.float32
        ).astype(jnp.bfloat16)
        q_buf[s, 2 * (g - 2)] = result[:, :HEAD_SIZE]
        q_buf[s, 2 * (g - 2) + 1] = result[:, HEAD_SIZE:]

    def project_last(s):
        q_buf[s, GROUP - 1] = jnp.dot(
            normed[s], weights_buf[GROUPS - 1, :, :HEAD_SIZE], preferred_element_type=jnp.float32
        ).astype(jnp.bfloat16)

    def make_beacons(s):
        part = pl.ds(pl.multiple_of(s * slots, slots), slots)
        made = jnp.dot(pooled[part, :], weights_buf[0], preferred_element_type=jnp.float32)
        block = beacon_rows(z * 2 + s, 1)
        block[...] = made.astype(jnp.bfloat16)
        send_up(block, 0, z)

    def await_beacons():
        for m in range(n_z - 1):

            @pl.when(m < z)
            def _():
                block = beacon_rows(2 * m, 2)
                remote(block, block, bs.at[0], br.at[0, m], x_peer).wait_recv()
                bias = live_bias.at[m]
                remote(bias, bias, bs.at[1], br.at[1, m], x_peer).wait_recv()

        mask_far()

    factor = math.log2(math.e) / math.sqrt(HEAD_SIZE)
    contract = (((1,), (1,)), ((), ()))

    def attend(s, j, which, width, count):
        query = q_buf[s, pl.ds(j, count)].reshape(count * tokens, HEAD_SIZE)
        far = lax.dot_general(
            query, beacons[:width, :HEAD_SIZE], contract, preferred_element_type=jnp.float32
        )
        near = lax.dot_general(
            query, kv_buf[s, :, :HEAD_SIZE], contract, preferred_element_type=jnp.float32
        )
        far = far * factor + span_bias[s, 0:1, :width]
        near = (near * factor).reshape(count, tokens, tokens) + raw_bias[s][None]
        near = near.reshape(count * tokens, tokens)
        top = jnp.maximum(
            jnp.max(far, axis=1, keepdims=True), jnp.max(near, axis=1, keepdims=True)
        )
        far = jnp.exp2(far - top)
        near = jnp.exp2(near - top)
        total = jnp.sum(far, axis=1, keepdims=True) + jnp.sum(near, axis=1, keepdims=True)
        mixed = jnp.dot(
            far.astype(jnp.bfloat16),
            beacons[:width, HEAD_SIZE:],
            preferred_element_type=jnp.float32,
        ) + jnp.dot(
            near.astype(jnp.bfloat16),
            kv_buf[s, :, HEAD_SIZE:],
            preferred_element_type=jnp.float32,
        )
        row = lax.broadcasted_iota(jnp.int32, (count, tokens, 1), 1)
        position = (z * 2 + s) * tokens + row.reshape(count * tokens, 1)
        scale = jnp.where(position < length, 1.0 / total, 0.0)
        made_out[which, pl.ds(j, count)] = (
            (mixed * scale).astype(jnp.bfloat16).reshape(count, tokens, HEAD_SIZE)
        )

    def heads(first, last):
        count = last - first
        for which, s in ((1, other_x), (0, x)):

            @pl.when(z == 0)
            def _():
                attend(s, first, which, pair, count)

            @pl.when(z > 0)
            def _():
                attend(s, first, which, n_z * pair, count)

            for j in range(first, last):
                (keep_copy, out_copy)[which](j).start()

    pltpu.make_async_copy(amount(PIECES), amount(PIECES), own_sem).wait()
    for f in range(AHEAD):
        launch(f)
    for i in range(STRIPS):
        norm_own(i)
    for p in Y_FIRST:
        begin(p)
    tick(0)
    pool(x)
    mask_near()
    tick(1)
    tick(2)
    norm_other(0)
    tick(3)
    tick(4)
    level_copy.wait_recv()
    own_live()
    tick(5)
    y_arrived(0)
    norm_other(1)
    tick(6)
    y_arrived(1)
    arrived(0)
    make_beacons(x)
    tick(7)
    y_arrived(2)
    tick(8)
    y_arrived(3)
    norm_other(2)
    arrived(1)
    project_kv(x)
    tick(9)
    y_arrived(4)
    tick(10)
    y_arrived(5)
    arrived(2)
    project_query(x, 2)
    tick(11)
    y_arrived(6)
    norm_other(3)
    pool(other_x)
    make_beacons(other_x)
    project_kv(other_x)
    tick(12)
    y_arrived(7)
    project_query(other_x, 2)
    tick(13)
    y_arrived(8)
    await_beacons()
    heads(0, 2)
    arrived(3)
    project_query(x, 3)
    project_query(other_x, 3)
    heads(2, 4)
    arrived(4)
    project_query(x, 4)
    project_query(other_x, 4)
    heads(4, 6)
    tick(14)
    arrived(5)
    project_last(x)
    project_last(other_x)
    heads(6, 7)
    pltpu.make_async_copy(half(x), half(x), keep_sem).wait()
    remote(half(other_x), half(other_x), os_, or_, x_peer).wait()
    remote(amount(PIECES), amount(PIECES), xs, xr.at[0], x_peer).wait_send()
    every = amount((PIECES - len(Y_FIRST)) * 2 * n_z + 2 * len(Y_FIRST))
    remote(every, every, ys, yr.at[0], y_peer).wait_send()
    every = amount(PIECES * 2 * n_ctx)
    remote(every, every, cs, cr.at[0], mate).wait_send()
    for m in range(n_z):

        @pl.when(has_up & (z == m))
        def _():
            every = amount(len(FLOWS) * 2 * (m + 1))
            remote(every, every, zu, zr.at[0, 0], z_up).wait_send()
            every = beacons.at[0 : (n_z - 1 - m) * pair, :]
            remote(every, every, bs.at[0], br.at[0, 0], z_up).wait_send()
            every = live_bias.at[0 : n_z - 1 - m]
            remote(every, every, bs.at[1], br.at[1, 0], z_up).wait_send()

        @pl.when(has_down & (z == m))
        def _():
            every = amount(len(FLOWS) * 2 * (n_z - m))
            remote(every, every, zd, zr.at[0, 0], z_down).wait_send()

    remote(hidden_hbm, hidden.at[1], hs, hr.at[0], x_peer).wait_send()
    level_copy.wait_send()


def on_device_paired(
    n_dp,
    n_ctx,
    hidden_in,
    norm_gain,
    w_query,
    w_key,
    value_weight,
    marker_key_weight,
    marker_value_weight,
    ratio_level,
    hist_len,
):
    tokens, width = hidden_in.shape[1:]
    slots = tokens // 4
    n_z = n_ctx // 2
    flows = len(FLOWS)
    dma = pltpu.SemaphoreType.DMA
    vmem = pl.BlockSpec(memory_space=pltpu.VMEM)
    smem = pl.BlockSpec(memory_space=pltpu.SMEM)
    hbm = pl.BlockSpec(memory_space=pl.ANY)
    bf16 = jnp.bfloat16
    result = pl.pallas_call(
        functools.partial(sublayer_kernel, n_dp, n_ctx),
        out_shape=jax.ShapeDtypeStruct((tokens, QUERY_HEADS * HEAD_SIZE), bf16),
        in_specs=[smem, smem, hbm, vmem] + [hbm] * 5,
        out_specs=hbm,
        scratch_shapes=[
            pltpu.VMEM((2, tokens, width), bf16),
            pltpu.VMEM((2, 8, 128), jnp.int32),
            pltpu.VMEM((GROUPS, width, 2 * HEAD_SIZE), bf16),
            pltpu.VMEM((2, tokens, width), bf16),
            pltpu.VMEM((2 * slots, width), bf16),
            pltpu.VMEM((n_ctx * slots, 2 * HEAD_SIZE), bf16),
            pltpu.VMEM((n_z, 8, 2 * slots), jnp.float32),
            pltpu.VMEM((2, tokens, 2 * HEAD_SIZE), bf16),
            pltpu.VMEM((2, GROUP, tokens, HEAD_SIZE), bf16),
            pltpu.VMEM((2, 8, n_ctx * slots), jnp.float32),
            pltpu.VMEM((2, tokens, tokens), jnp.float32),
            pltpu.VMEM((2, GROUP, tokens, HEAD_SIZE), bf16),
            dma,
            dma((STRIPS,)),
            dma,
            dma((PIECES,)),
            dma,
            dma,
            dma((flows, n_z)),
            dma,
            dma((PIECES,)),
            dma,
            dma((GROUPS,)),
            dma,
            dma((STRIPS,)),
            dma,
            dma,
            dma((2,)),
            dma((2, n_z)),
            dma,
            dma,
            dma,
        ],
        compiler_params=pltpu.CompilerParams(
            collective_id=0, has_side_effects=True, vmem_limit_bytes=56 * 2**20
        ),
    )(
        hist_len,
        ratio_level,
        hidden_in[0],
        norm_gain,
        w_query,
        w_key,
        value_weight,
        marker_key_weight,
        marker_value_weight,
    )
    return result[None]


def solution(mesh):
    n_dp, n_ctx = mesh.shape["dp"], mesh.shape["ctx"]

    def body(*args):
        tokens, rows = args[0].shape[1], args[2].shape[0]
        if rows % 16 == 0 and tokens == 256 and n_dp == 4 and n_ctx % 2 == 0 and n_ctx > 2:
            return on_device_paired(n_dp, n_ctx, *args)
        return on_device(*args)

    return jax.shard_map(
        body,
        mesh=mesh,
        in_specs=(
            P("dp", "ctx", None),
            P(),
            P(("dp", "ctx"), None),
            P(("dp", "ctx"), None),
            P(("dp", "ctx"), None),
            P(("dp", "ctx"), None),
            P(("dp", "ctx"), None),
            P("dp", "ctx"),
            P("dp"),
        ),
        out_specs=P("dp", "ctx", None),
        check_vma=False,
    )
```

```python
import functools
import math

import jax
import jax.numpy as jnp
from jax import lax
from jax.experimental import pallas as pl
from jax.experimental.pallas import tpu as pltpu
from jax.sharding import PartitionSpec as P

QUERY_HEADS = 14
KEY_VALUE_HEADS = 2
HEAD_SIZE = 128


eps_norm = 1e-06
negative_filler = -1e30


def norm_rows(tokens, norm_gain):
    values = tokens.astype(jnp.float32)
    factor = lax.rsqrt(jnp.mean(values * values, axis=-1, keepdims=True) + eps_norm)
    return (values * factor * norm_gain).astype(jnp.bfloat16)


def window_table(span_level, begin_offset, length, token_rows, marker_slot_count):
    stride = (4 * jnp.power(2, span_level)).astype(jnp.int32)
    live_count = token_rows // stride
    slot_ids = lax.broadcasted_iota(jnp.int32, (marker_slot_count, token_rows), 0)
    pos_ids = lax.broadcasted_iota(jnp.int32, (marker_slot_count, token_rows), 1)
    inside = (
        (pos_ids // stride == slot_ids)
        & (slot_ids < live_count)
        & (begin_offset + pos_ids < length)
    )
    slot_col = jnp.arange(marker_slot_count, dtype=jnp.int32)
    live_slot = (slot_col < live_count) & (begin_offset + slot_col * stride < length)
    return (inside, live_slot)


def pool_rows(inside, normed):
    window_sum = jnp.dot(inside.astype(jnp.bfloat16), normed, preferred_element_type=jnp.float32)
    window_size = jnp.sum(inside.astype(jnp.float32), axis=1)
    return (window_sum / jnp.maximum(window_size, 1.0)[:, None]).astype(jnp.bfloat16)


def raw_attention(query_matrix, key_matrix, value_matrix, begin_offset, length, score_scale):
    token_rows = key_matrix.shape[0]
    scores = (
        jnp.einsum("kgtd,skd->kgts", query_matrix, key_matrix, preferred_element_type=jnp.float32)
        * score_scale
    )
    positions = jnp.arange(token_rows, dtype=jnp.int32)
    visible = (positions[None, :] <= positions[:, None]) & (
        begin_offset + positions[None, :] < length
    )
    scores = jnp.where(visible, scores, negative_filler)
    top_score = jnp.max(scores, axis=-1)
    weights = jnp.where(visible, jnp.exp(scores - top_score[..., None]), 0.0)
    weight_sum = jnp.sum(weights, axis=-1)
    weighted = jnp.einsum(
        "kgts,skd->kgtd",
        weights.astype(jnp.bfloat16),
        value_matrix,
        preferred_element_type=jnp.float32,
    )
    return (top_score, weight_sum, weighted)


def beacon_update(
    carry_state,
    query_matrix,
    limit,
    marker_key_rows,
    marker_value_rows,
    beacon_live,
    marker_slot_count,
    score_scale,
):
    row_total = marker_key_rows.shape[0]
    span_of = jnp.arange(row_total, dtype=jnp.int32) // marker_slot_count
    visible = (beacon_live > 0) & (span_of < limit)

    def compute(state):
        running, weight_sum, weighted = state
        scores = (
            jnp.einsum(
                "kgtd,skd->kgts", query_matrix, marker_key_rows, preferred_element_type=jnp.float32
            )
            * score_scale
        )
        scores = jnp.where(visible, scores, negative_filler)
        new_top = jnp.maximum(running, jnp.max(scores, axis=-1))
        weights = jnp.where(visible, jnp.exp(scores - new_top[..., None]), 0.0)
        added = jnp.einsum(
            "kgts,skd->kgtd",
            weights.astype(jnp.bfloat16),
            marker_value_rows,
            preferred_element_type=jnp.float32,
        )
        return (new_top, jnp.sum(weights, axis=-1), added)

    def unchanged(state):
        return state

    return lax.cond(jnp.any(visible), compute, unchanged, carry_state)


def on_device(
    hidden_in,
    norm_gain,
    w_query,
    w_key,
    value_weight,
    marker_key_weight,
    marker_value_weight,
    ratio_level,
    hist_len,
):
    token_rows = hidden_in.shape[1]
    marker_slot_count = token_rows // 4
    my_span = lax.axis_index("ctx")
    begin_offset = my_span * token_rows
    length = hist_len[0]
    query_group_count = QUERY_HEADS // KEY_VALUE_HEADS
    score_scale = 1.0 / math.sqrt(HEAD_SIZE)
    normed = norm_rows(hidden_in[0], norm_gain)
    inside, live_slot = window_table(
        ratio_level[0, 0], begin_offset, length, token_rows, marker_slot_count
    )
    pooled = pool_rows(inside, normed)
    local_part = (
        lax.all_gather(w_query, "ctx", axis=0, tiled=True),
        lax.all_gather(w_key, "ctx", axis=0, tiled=True),
        lax.all_gather(value_weight, "ctx", axis=0, tiled=True),
        lax.all_gather(marker_key_weight, "ctx", axis=0, tiled=True),
        lax.all_gather(marker_value_weight, "ctx", axis=0, tiled=True),
    )
    segment_list = (
        lax.all_gather(local_part[0], "dp", axis=0, tiled=True),
        lax.all_gather(local_part[1], "dp", axis=0, tiled=True),
        lax.all_gather(local_part[2], "dp", axis=0, tiled=True),
        lax.all_gather(local_part[3], "dp", axis=0, tiled=True),
        lax.all_gather(local_part[4], "dp", axis=0, tiled=True),
    )
    flattened_query = jnp.dot(normed, segment_list[0], preferred_element_type=jnp.float32).astype(
        jnp.bfloat16
    )
    query_matrix = flattened_query.reshape(
        token_rows, KEY_VALUE_HEADS, query_group_count, HEAD_SIZE
    ).transpose(1, 2, 0, 3)
    key_matrix = (
        jnp.dot(normed, segment_list[1], preferred_element_type=jnp.float32)
        .astype(jnp.bfloat16)
        .reshape(token_rows, KEY_VALUE_HEADS, HEAD_SIZE)
    )
    value_matrix = (
        jnp.dot(normed, segment_list[2], preferred_element_type=jnp.float32)
        .astype(jnp.bfloat16)
        .reshape(token_rows, KEY_VALUE_HEADS, HEAD_SIZE)
    )
    marker_key_rows = jnp.dot(pooled, segment_list[3], preferred_element_type=jnp.float32).astype(
        jnp.bfloat16
    )
    marker_value_rows = jnp.dot(pooled, segment_list[4], preferred_element_type=jnp.float32).astype(
        jnp.bfloat16
    )
    raw_top, raw_sum, raw_weighted = raw_attention(
        query_matrix, key_matrix, value_matrix, begin_offset, length, score_scale
    )
    halved_rows = token_rows // 2
    first_q = query_matrix[:, :, :halved_rows]
    second_q = query_matrix[:, :, halved_rows:]
    empty_state = (
        jnp.full((KEY_VALUE_HEADS, query_group_count, halved_rows), negative_filler, jnp.float32),
        jnp.zeros((KEY_VALUE_HEADS, query_group_count, halved_rows), jnp.float32),
        jnp.zeros((KEY_VALUE_HEADS, query_group_count, halved_rows, HEAD_SIZE), jnp.float32),
    )
    segment_list = (
        lax.all_gather(marker_key_rows, "ctx", axis=0, tiled=True),
        lax.all_gather(marker_value_rows, "ctx", axis=0, tiled=True),
        lax.all_gather(live_slot.astype(jnp.bfloat16), "ctx", axis=0, tiled=True),
    )
    segment_keys = segment_list[0].reshape(-1, KEY_VALUE_HEADS, HEAD_SIZE)
    segment_values = segment_list[1].reshape(-1, KEY_VALUE_HEADS, HEAD_SIZE)
    first_state = beacon_update(
        empty_state,
        first_q,
        my_span,
        segment_keys,
        segment_values,
        segment_list[2],
        marker_slot_count,
        score_scale,
    )
    second_state = beacon_update(
        empty_state,
        second_q,
        my_span,
        segment_keys,
        segment_values,
        segment_list[2],
        marker_slot_count,
        score_scale,
    )
    first_state, second_state = (first_state, second_state)
    beacon_top = jnp.concatenate([first_state[0], second_state[0]], axis=2)
    beacon_sum = jnp.concatenate([first_state[1], second_state[1]], axis=2)
    beacon_weighted = jnp.concatenate([first_state[2], second_state[2]], axis=2)
    joint_top = jnp.maximum(raw_top, beacon_top)
    raw_factor = jnp.exp(raw_top - joint_top)
    beacon_factor = jnp.exp(beacon_top - joint_top)
    weight_sum = raw_sum * raw_factor + beacon_sum * beacon_factor
    weighted = raw_weighted * raw_factor[..., None] + beacon_weighted * beacon_factor[..., None]
    result = weighted / jnp.where(weight_sum > 0, weight_sum, 1.0)[..., None]
    result = result.transpose(2, 0, 1, 3).reshape(token_rows, QUERY_HEADS * HEAD_SIZE)
    valid = begin_offset + jnp.arange(token_rows, dtype=jnp.int32) < length
    result = jnp.where(valid[:, None], result, 0.0).astype(jnp.bfloat16)
    return result[None]


GROUP = QUERY_HEADS // KEY_VALUE_HEADS
PIECES = 4 + GROUP
GROUPS = (PIECES + 1) // 2
AHEAD = 5
Y_FIRST = (PIECES - 2, PIECES - 1)
FLOWS = [(p, 0) for p in range(PIECES)] + [(p, 1) for p in Y_FIRST]
STRIPS = 4
MESH = pl.DeviceIdType.MESH


def sublayer_kernel(
    n_dp,
    n_ctx,
    length_ref,
    level_ref,
    hidden_hbm,
    gain_ref,
    wq_ref,
    wk_ref,
    wv_ref,
    mk_ref,
    mv_ref,
    out_ref,
    hidden,
    levels,
    weights_buf,
    normed,
    pooled,
    beacons,
    live_bias,
    kv_buf,
    q_buf,
    span_bias,
    raw_bias,
    made_out,
    own_sem,
    load_sem,
    xs,
    xr,
    zu,
    zd,
    zr,
    ys,
    yr,
    cs,
    cr,
    hs,
    hr,
    ls,
    lr,
    bs,
    br,
    os_,
    or_,
    keep_sem,
):
    tokens = hidden_hbm.shape[0]
    rows = wq_ref.shape[0]
    slots = tokens // 4
    n_z = n_ctx // 2
    pair = 2 * slots
    dp = lax.axis_index("dp")
    ctx = lax.axis_index("ctx")
    z, x = ctx // 2, lax.rem(ctx, 2)
    other_x = 1 - x
    x_peer = (dp, z * 2 + other_x)
    y_dp = lax.rem(dp + n_dp // 2, n_dp)
    y_peer = (y_dp, ctx)
    mate = (dp + 1 - 2 * lax.rem(dp, 2), ctx)
    has_up, has_down = z + 1 < n_z, z > 0
    z_up = (dp, lax.rem(z + 1, n_z) * 2 + x)
    z_down = (dp, lax.rem(z + n_z - 1, n_z) * 2 + x)

    barrier = pltpu.get_barrier_semaphore()

    def greet(peer):
        pl.semaphore_signal(barrier, inc=1, device_id=peer, device_id_type=MESH)

    for peer in (x_peer, y_peer, mate):
        greet(peer)

    @pl.when(has_up)
    def _():
        greet(z_up)

    @pl.when(has_down)
    def _():
        greet(z_down)

    def remote(source, target, send, recv, peer):
        return pltpu.make_async_remote_copy(
            src_ref=source,
            dst_ref=target,
            send_sem=send,
            recv_sem=recv,
            device_id=peer,
            device_id_type=MESH,
        )

    strip = tokens // STRIPS

    def load_copy(i):
        part = pl.ds(i * strip, strip)
        return pltpu.make_async_copy(
            hidden_hbm.at[part, :], hidden.at[0, part, :], load_sem.at[i]
        )

    for i in range(STRIPS):
        load_copy(i).start()

    def piece_source(p, head):
        if p < 4:
            ref = (mk_ref, mv_ref, wk_ref, wv_ref)[p]
            column = head * HEAD_SIZE
        else:
            ref = wq_ref
            column = (head * GROUP + p - 4) * HEAD_SIZE
        return ref.at[:, pl.ds(pl.multiple_of(column, HEAD_SIZE), HEAD_SIZE)]

    def piece_rows(p, start, count):
        return weights_buf.at[
            p // 2,
            pl.ds(pl.multiple_of(start * rows, 16), count * rows),
            pl.ds((p % 2) * HEAD_SIZE, HEAD_SIZE),
        ]

    me = dp * n_ctx + ctx

    def amount(blocks):
        for a in range(1, GROUPS + 1):
            if blocks % (2 * a) == 0 and blocks // (2 * a) <= n_dp * n_ctx:
                return weights_buf.at[0:a, 0 : blocks // (2 * a) * rows, :]
        return weights_buf.at[0, 0 : blocks * rows, 0:HEAD_SIZE]

    def own_copy(p):
        return pltpu.make_async_copy(piece_source(p, x), piece_rows(p, me, 1), own_sem)

    def x_copy(p):
        return remote(piece_source(p, other_x), piece_rows(p, me, 1), xs, xr.at[p], x_peer)

    for p in range(PIECES):
        own_copy(p).start()

    for m in range(1, n_z):

        @pl.when(z < m)
        def _():
            beacons[m * pair : (m + 1) * pair, :] = jnp.zeros(
                (pair, 2 * HEAD_SIZE), jnp.bfloat16
            )
            live_bias[m] = jnp.full((8, pair), negative_filler, jnp.float32)

    levels[x] = jnp.broadcast_to(level_ref[0, 0], (8, 128))
    length = length_ref[0]

    pl.semaphore_wait(
        barrier, 3 + has_up.astype(jnp.int32) + has_down.astype(jnp.int32)
    )

    def z_copy(f, source, step):
        p, column = FLOWS[f]
        block = piece_rows(p, (dp, y_dp)[column] * n_ctx + source * 2, 2)
        sends = zu if step > 0 else zd
        peer = z_up if step > 0 else z_down
        return remote(block, block, sends, zr.at[f, source], peer)

    def y_copy(p, source):
        block = piece_rows(p, dp * n_ctx + source * 2, 2)
        return remote(block, block, ys, yr.at[p], y_peer)

    def c_copy(p, which):
        block = piece_rows(p, (dp, y_dp)[which] * n_ctx, n_ctx)
        return remote(block, block, cs, cr.at[p // 2], mate)

    def begin(p):
        x_copy(p).wait_recv()
        y_copy(p, z).start()

    def launch(f):
        p, column = FLOWS[f]
        if column == 1:
            y_copy(p, z).wait_recv()
        elif p not in Y_FIRST:
            begin(p)

        @pl.when(has_up)
        def _():
            z_copy(f, z, 1).start()

        @pl.when(has_down)
        def _():
            z_copy(f, z, -1).start()

    def relay(f, d):
        p, column = FLOWS[f]
        spread = column == 0 and p not in Y_FIRST

        @pl.when(z - d >= 0)
        def _():
            z_copy(f, z - d, 1).wait_recv()
            if spread:
                y_copy(p, z - d).start()

            @pl.when(has_up)
            def _():
                z_copy(f, z - d, 1).start()

        @pl.when(z + d < n_z)
        def _():
            z_copy(f, z + d, -1).wait_recv()
            if spread:
                y_copy(p, z + d).start()

            @pl.when(has_down)
            def _():
                z_copy(f, z + d, -1).start()

        if d == n_z - 1:
            c_copy(p, column).start()

    def tick(t):
        for d in range(1, n_z):
            f = t - d + 1
            if 0 <= f < len(FLOWS):
                relay(f, d)
        if t + AHEAD < len(FLOWS):
            launch(t + AHEAD)

    def y_arrived(p):
        if p not in Y_FIRST:
            block = piece_rows(p, y_dp * n_ctx, n_ctx)
            remote(block, block, ys, yr.at[p], y_peer).wait_recv()
            c_copy(p, 1).start()

    def arrived(g):
        last = HEAD_SIZE * (1 + min(1, PIECES - 1 - 2 * g))
        block = weights_buf.at[g, 0 : 2 * n_ctx * rows, 0:last]
        remote(block, block, cs, cr.at[g], mate).wait_recv()

    def hidden_copy(i):
        part = pl.ds(i * strip, strip)
        return remote(
            hidden_hbm.at[part, :], hidden.at[1, part, :], hs, hr.at[i], x_peer
        )

    level_copy = remote(levels.at[x], levels.at[x], ls, lr, x_peer)

    def beacon_rows(first, count):
        return beacons.at[pl.ds(pl.multiple_of(first * slots, slots), count * slots), :]

    def send_up(source, kind, level):
        for d in range(1, n_z):

            @pl.when(z + d < n_z)
            def _():
                peer = (dp, lax.rem(z + d, n_z) * 2 + x)
                remote(source, source, bs.at[kind], br.at[kind, level], peer).start()

    def head_columns(head, j):
        return pl.ds(pl.multiple_of((head * GROUP + j) * HEAD_SIZE, HEAD_SIZE), HEAD_SIZE)

    def out_copy(j):
        return remote(
            made_out.at[1, j], out_ref.at[:, head_columns(x, j)], os_, or_, x_peer
        )

    def keep_copy(j):
        return pltpu.make_async_copy(
            made_out.at[0, j], out_ref.at[:, head_columns(x, j)], keep_sem
        )

    def half(head):
        width = GROUP * HEAD_SIZE
        return out_ref.at[:, pl.ds(pl.multiple_of(head * width, HEAD_SIZE), width)]

    for p in range(PIECES):
        x_copy(p).start()
    level_copy.start()
    for i in range(STRIPS):
        hidden_copy(i).start()

    gain = gain_ref[...][None, :]

    def norm_strip(i, which, slot):
        def body(k, carry):
            part = pl.ds(pl.multiple_of(i * strip + k * 16, 16), 16)
            values = hidden[which, part, :].astype(jnp.float32)
            factor = lax.rsqrt(jnp.mean(values * values, axis=-1, keepdims=True) + eps_norm)
            normed[slot, part, :] = (values * factor * gain).astype(jnp.bfloat16)
            return carry

        lax.fori_loop(0, strip // 16, body, 0)

    def norm_own(i):
        load_copy(i).wait()
        norm_strip(i, 0, x)

    def norm_other(i):
        hidden_copy(i).wait_recv()
        norm_strip(i, 1, other_x)

    lane = lax.broadcasted_iota(jnp.int32, (1, pair), 1)
    slot_id = lax.rem(lane, slots)
    sub = lane // slots

    def stride_of(level):
        return jnp.where(
            level == 0, 4, jnp.where(level == 1, 8, jnp.where(level == 2, 16, 32))
        )

    def own_live():
        level = jnp.where(sub == 0, levels[0, 0:1, :], levels[1, 0:1, :])
        stride = stride_of(level)
        owner = 2 * z + sub
        live = (slot_id * stride < tokens) & (owner * tokens + slot_id * stride < length)
        live_bias[z] = jnp.broadcast_to(jnp.where(live, 0.0, negative_filler), (8, pair))
        send_up(live_bias.at[z], 1, z)

    def mask_far():
        for s in range(2):
            for m in range(n_z):
                seen = (2 * m + sub) < (2 * z + s)
                span_bias[s, :, m * pair : (m + 1) * pair] = jnp.where(
                    seen, live_bias[m], negative_filler
                )

    def mask_near():
        for s in range(2):
            row_id = lax.broadcasted_iota(jnp.int32, (tokens, tokens), 0)
            col_id = lax.broadcasted_iota(jnp.int32, (tokens, tokens), 1)
            seen = (col_id <= row_id) & ((z * 2 + s) * tokens + col_id < length)
            raw_bias[s] = jnp.where(seen, 0.0, negative_filler)

    def pool(s):
        span = z * 2 + s
        level = jnp.broadcast_to(levels[s, 0:1, :], (slots, 128))
        stride = stride_of(level)
        slot = lax.broadcasted_iota(jnp.int32, (slots, 128), 0)
        parts = []
        for b in range(tokens // 128):
            pos = lax.broadcasted_iota(jnp.int32, (slots, 128), 1) + b * 128
            inside = (
                (pos >= slot * stride)
                & (pos < (slot + 1) * stride)
                & (span * tokens + pos < length)
            )
            parts.append(jnp.where(inside, 1.0, 0.0))
        inside = jnp.concatenate(parts, axis=1)
        scale = 1.0 / jnp.maximum(jnp.sum(inside, axis=1, keepdims=True), 1.0)
        table = inside.astype(jnp.bfloat16)
        width = normed.shape[2] // 4

        def body(i, carry):
            cols = pl.ds(pl.multiple_of(i * width, 128), width)
            total = jnp.dot(table, normed[s, :, cols], preferred_element_type=jnp.float32)
            pooled[pl.ds(pl.multiple_of(s * slots, slots), slots), cols] = (
                total * scale
            ).astype(jnp.bfloat16)
            return carry

        lax.fori_loop(0, 4, body, 0)

    def project_kv(s):
        kv_buf[s] = jnp.dot(
            normed[s], weights_buf[1], preferred_element_type=jnp.float32
        ).astype(jnp.bfloat16)

    def project_query(s, g):
        result = jnp.dot(
            normed[s], weights_buf[g], preferred_element_type=jnp.float32
        ).astype(jnp.bfloat16)
        q_buf[s, 2 * (g - 2)] = result[:, :HEAD_SIZE]
        q_buf[s, 2 * (g - 2) + 1] = result[:, HEAD_SIZE:]

    def project_last(s):
        q_buf[s, GROUP - 1] = jnp.dot(
            normed[s], weights_buf[GROUPS - 1, :, :HEAD_SIZE], preferred_element_type=jnp.float32
        ).astype(jnp.bfloat16)

    def make_beacons(s):
        part = pl.ds(pl.multiple_of(s * slots, slots), slots)
        made = jnp.dot(pooled[part, :], weights_buf[0], preferred_element_type=jnp.float32)
        block = beacon_rows(z * 2 + s, 1)
        block[...] = made.astype(jnp.bfloat16)
        send_up(block, 0, z)

    def await_beacons():
        for m in range(n_z - 1):

            @pl.when(m < z)
            def _():
                block = beacon_rows(2 * m, 2)
                remote(block, block, bs.at[0], br.at[0, m], x_peer).wait_recv()
                bias = live_bias.at[m]
                remote(bias, bias, bs.at[1], br.at[1, m], x_peer).wait_recv()

        mask_far()

    factor = math.log2(math.e) / math.sqrt(HEAD_SIZE)
    contract = (((1,), (1,)), ((), ()))

    def attend(s, j, which, width, count):
        query = q_buf[s, pl.ds(j, count)].reshape(count * tokens, HEAD_SIZE)
        far = lax.dot_general(
            query, beacons[:width, :HEAD_SIZE], contract, preferred_element_type=jnp.float32
        )
        near = lax.dot_general(
            query, kv_buf[s, :, :HEAD_SIZE], contract, preferred_element_type=jnp.float32
        )
        far = far * factor + span_bias[s, 0:1, :width]
        near = (near * factor).reshape(count, tokens, tokens) + raw_bias[s][None]
        near = near.reshape(count * tokens, tokens)
        top = jnp.maximum(
            jnp.max(far, axis=1, keepdims=True), jnp.max(near, axis=1, keepdims=True)
        )
        far = jnp.exp2(far - top)
        near = jnp.exp2(near - top)
        total = jnp.sum(far, axis=1, keepdims=True) + jnp.sum(near, axis=1, keepdims=True)
        mixed = jnp.dot(
            far.astype(jnp.bfloat16),
            beacons[:width, HEAD_SIZE:],
            preferred_element_type=jnp.float32,
        ) + jnp.dot(
            near.astype(jnp.bfloat16),
            kv_buf[s, :, HEAD_SIZE:],
            preferred_element_type=jnp.float32,
        )
        row = lax.broadcasted_iota(jnp.int32, (count, tokens, 1), 1)
        position = (z * 2 + s) * tokens + row.reshape(count * tokens, 1)
        scale = jnp.where(position < length, 1.0 / total, 0.0)
        made_out[which, pl.ds(j, count)] = (
            (mixed * scale).astype(jnp.bfloat16).reshape(count, tokens, HEAD_SIZE)
        )

    def heads(first, last):
        count = last - first
        for which, s in ((1, other_x), (0, x)):

            @pl.when(z == 0)
            def _():
                attend(s, first, which, pair, count)

            @pl.when(z > 0)
            def _():
                attend(s, first, which, n_z * pair, count)

            for j in range(first, last):
                (keep_copy, out_copy)[which](j).start()

    pltpu.make_async_copy(amount(PIECES), amount(PIECES), own_sem).wait()
    for f in range(AHEAD):
        launch(f)
    for i in range(STRIPS):
        norm_own(i)
    for p in Y_FIRST:
        begin(p)
    tick(0)
    pool(x)
    mask_near()
    tick(1)
    tick(2)
    norm_other(0)
    tick(3)
    tick(4)
    level_copy.wait_recv()
    own_live()
    tick(5)
    y_arrived(0)
    norm_other(1)
    tick(6)
    y_arrived(1)
    arrived(0)
    make_beacons(x)
    tick(7)
    y_arrived(2)
    tick(8)
    y_arrived(3)
    norm_other(2)
    arrived(1)
    project_kv(x)
    tick(9)
    y_arrived(4)
    tick(10)
    y_arrived(5)
    arrived(2)
    project_query(x, 2)
    tick(11)
    y_arrived(6)
    norm_other(3)
    pool(other_x)
    make_beacons(other_x)
    project_kv(other_x)
    tick(12)
    y_arrived(7)
    project_query(other_x, 2)
    arrived(3)
    project_query(x, 3)
    project_query(other_x, 3)
    tick(13)
    y_arrived(8)
    await_beacons()
    heads(0, 2)
    heads(2, 4)
    arrived(4)
    project_query(x, 4)
    project_query(other_x, 4)
    heads(4, 6)
    tick(14)
    arrived(5)
    project_last(x)
    project_last(other_x)
    heads(6, 7)
    pltpu.make_async_copy(half(x), half(x), keep_sem).wait()
    remote(half(other_x), half(other_x), os_, or_, x_peer).wait()
    remote(amount(PIECES), amount(PIECES), xs, xr.at[0], x_peer).wait_send()
    every = amount((PIECES - len(Y_FIRST)) * 2 * n_z + 2 * len(Y_FIRST))
    remote(every, every, ys, yr.at[0], y_peer).wait_send()
    every = amount(PIECES * 2 * n_ctx)
    remote(every, every, cs, cr.at[0], mate).wait_send()
    for m in range(n_z):

        @pl.when(has_up & (z == m))
        def _():
            every = amount(len(FLOWS) * 2 * (m + 1))
            remote(every, every, zu, zr.at[0, 0], z_up).wait_send()
            every = beacons.at[0 : (n_z - 1 - m) * pair, :]
            remote(every, every, bs.at[0], br.at[0, 0], z_up).wait_send()
            every = live_bias.at[0 : n_z - 1 - m]
            remote(every, every, bs.at[1], br.at[1, 0], z_up).wait_send()

        @pl.when(has_down & (z == m))
        def _():
            every = amount(len(FLOWS) * 2 * (n_z - m))
            remote(every, every, zd, zr.at[0, 0], z_down).wait_send()

    remote(hidden_hbm, hidden.at[1], hs, hr.at[0], x_peer).wait_send()
    level_copy.wait_send()


def on_device_paired(
    n_dp,
    n_ctx,
    hidden_in,
    norm_gain,
    w_query,
    w_key,
    value_weight,
    marker_key_weight,
    marker_value_weight,
    ratio_level,
    hist_len,
):
    tokens, width = hidden_in.shape[1:]
    slots = tokens // 4
    n_z = n_ctx // 2
    flows = len(FLOWS)
    dma = pltpu.SemaphoreType.DMA
    vmem = pl.BlockSpec(memory_space=pltpu.VMEM)
    smem = pl.BlockSpec(memory_space=pltpu.SMEM)
    hbm = pl.BlockSpec(memory_space=pl.ANY)
    bf16 = jnp.bfloat16
    result = pl.pallas_call(
        functools.partial(sublayer_kernel, n_dp, n_ctx),
        out_shape=jax.ShapeDtypeStruct((tokens, QUERY_HEADS * HEAD_SIZE), bf16),
        in_specs=[smem, smem, hbm, vmem] + [hbm] * 5,
        out_specs=hbm,
        scratch_shapes=[
            pltpu.VMEM((2, tokens, width), bf16),
            pltpu.VMEM((2, 8, 128), jnp.int32),
            pltpu.VMEM((GROUPS, width, 2 * HEAD_SIZE), bf16),
            pltpu.VMEM((2, tokens, width), bf16),
            pltpu.VMEM((2 * slots, width), bf16),
            pltpu.VMEM((n_ctx * slots, 2 * HEAD_SIZE), bf16),
            pltpu.VMEM((n_z, 8, 2 * slots), jnp.float32),
            pltpu.VMEM((2, tokens, 2 * HEAD_SIZE), bf16),
            pltpu.VMEM((2, GROUP, tokens, HEAD_SIZE), bf16),
            pltpu.VMEM((2, 8, n_ctx * slots), jnp.float32),
            pltpu.VMEM((2, tokens, tokens), jnp.float32),
            pltpu.VMEM((2, GROUP, tokens, HEAD_SIZE), bf16),
            dma,
            dma((STRIPS,)),
            dma,
            dma((PIECES,)),
            dma,
            dma,
            dma((flows, n_z)),
            dma,
            dma((PIECES,)),
            dma,
            dma((GROUPS,)),
            dma,
            dma((STRIPS,)),
            dma,
            dma,
            dma((2,)),
            dma((2, n_z)),
            dma,
            dma,
            dma,
        ],
        compiler_params=pltpu.CompilerParams(
            collective_id=0, has_side_effects=True, vmem_limit_bytes=56 * 2**20
        ),
    )(
        hist_len,
        ratio_level,
        hidden_in[0],
        norm_gain,
        w_query,
        w_key,
        value_weight,
        marker_key_weight,
        marker_value_weight,
    )
    return result[None]


def solution(mesh):
    n_dp, n_ctx = mesh.shape["dp"], mesh.shape["ctx"]

    def body(*args):
        tokens, rows = args[0].shape[1], args[2].shape[0]
        if rows % 16 == 0 and tokens == 256 and n_dp == 4 and n_ctx % 2 == 0 and n_ctx > 2:
            return on_device_paired(n_dp, n_ctx, *args)
        return on_device(*args)

    return jax.shard_map(
        body,
        mesh=mesh,
        in_specs=(
            P("dp", "ctx", None),
            P(),
            P(("dp", "ctx"), None),
            P(("dp", "ctx"), None),
            P(("dp", "ctx"), None),
            P(("dp", "ctx"), None),
            P(("dp", "ctx"), None),
            P("dp", "ctx"),
            P("dp"),
        ),
        out_specs=P("dp", "ctx", None),
        check_vma=False,
    )
```

```python
import functools
import math

import jax
import jax.numpy as jnp
from jax import lax
from jax.experimental import pallas as pl
from jax.experimental.pallas import tpu as pltpu
from jax.sharding import PartitionSpec as P

QUERY_HEADS = 14
KEY_VALUE_HEADS = 2
HEAD_SIZE = 128


eps_norm = 1e-06
negative_filler = -1e30


def norm_rows(tokens, norm_gain):
    values = tokens.astype(jnp.float32)
    factor = lax.rsqrt(jnp.mean(values * values, axis=-1, keepdims=True) + eps_norm)
    return (values * factor * norm_gain).astype(jnp.bfloat16)


def window_table(span_level, begin_offset, length, token_rows, marker_slot_count):
    stride = (4 * jnp.power(2, span_level)).astype(jnp.int32)
    live_count = token_rows // stride
    slot_ids = lax.broadcasted_iota(jnp.int32, (marker_slot_count, token_rows), 0)
    pos_ids = lax.broadcasted_iota(jnp.int32, (marker_slot_count, token_rows), 1)
    inside = (
        (pos_ids // stride == slot_ids)
        & (slot_ids < live_count)
        & (begin_offset + pos_ids < length)
    )
    slot_col = jnp.arange(marker_slot_count, dtype=jnp.int32)
    live_slot = (slot_col < live_count) & (begin_offset + slot_col * stride < length)
    return (inside, live_slot)


def pool_rows(inside, normed):
    window_sum = jnp.dot(inside.astype(jnp.bfloat16), normed, preferred_element_type=jnp.float32)
    window_size = jnp.sum(inside.astype(jnp.float32), axis=1)
    return (window_sum / jnp.maximum(window_size, 1.0)[:, None]).astype(jnp.bfloat16)


def raw_attention(query_matrix, key_matrix, value_matrix, begin_offset, length, score_scale):
    token_rows = key_matrix.shape[0]
    scores = (
        jnp.einsum("kgtd,skd->kgts", query_matrix, key_matrix, preferred_element_type=jnp.float32)
        * score_scale
    )
    positions = jnp.arange(token_rows, dtype=jnp.int32)
    visible = (positions[None, :] <= positions[:, None]) & (
        begin_offset + positions[None, :] < length
    )
    scores = jnp.where(visible, scores, negative_filler)
    top_score = jnp.max(scores, axis=-1)
    weights = jnp.where(visible, jnp.exp(scores - top_score[..., None]), 0.0)
    weight_sum = jnp.sum(weights, axis=-1)
    weighted = jnp.einsum(
        "kgts,skd->kgtd",
        weights.astype(jnp.bfloat16),
        value_matrix,
        preferred_element_type=jnp.float32,
    )
    return (top_score, weight_sum, weighted)


def beacon_update(
    carry_state,
    query_matrix,
    limit,
    marker_key_rows,
    marker_value_rows,
    beacon_live,
    marker_slot_count,
    score_scale,
):
    row_total = marker_key_rows.shape[0]
    span_of = jnp.arange(row_total, dtype=jnp.int32) // marker_slot_count
    visible = (beacon_live > 0) & (span_of < limit)

    def compute(state):
        running, weight_sum, weighted = state
        scores = (
            jnp.einsum(
                "kgtd,skd->kgts", query_matrix, marker_key_rows, preferred_element_type=jnp.float32
            )
            * score_scale
        )
        scores = jnp.where(visible, scores, negative_filler)
        new_top = jnp.maximum(running, jnp.max(scores, axis=-1))
        weights = jnp.where(visible, jnp.exp(scores - new_top[..., None]), 0.0)
        added = jnp.einsum(
            "kgts,skd->kgtd",
            weights.astype(jnp.bfloat16),
            marker_value_rows,
            preferred_element_type=jnp.float32,
        )
        return (new_top, jnp.sum(weights, axis=-1), added)

    def unchanged(state):
        return state

    return lax.cond(jnp.any(visible), compute, unchanged, carry_state)


def on_device(
    hidden_in,
    norm_gain,
    w_query,
    w_key,
    value_weight,
    marker_key_weight,
    marker_value_weight,
    ratio_level,
    hist_len,
):
    token_rows = hidden_in.shape[1]
    marker_slot_count = token_rows // 4
    my_span = lax.axis_index("ctx")
    begin_offset = my_span * token_rows
    length = hist_len[0]
    query_group_count = QUERY_HEADS // KEY_VALUE_HEADS
    score_scale = 1.0 / math.sqrt(HEAD_SIZE)
    normed = norm_rows(hidden_in[0], norm_gain)
    inside, live_slot = window_table(
        ratio_level[0, 0], begin_offset, length, token_rows, marker_slot_count
    )
    pooled = pool_rows(inside, normed)
    local_part = (
        lax.all_gather(w_query, "ctx", axis=0, tiled=True),
        lax.all_gather(w_key, "ctx", axis=0, tiled=True),
        lax.all_gather(value_weight, "ctx", axis=0, tiled=True),
        lax.all_gather(marker_key_weight, "ctx", axis=0, tiled=True),
        lax.all_gather(marker_value_weight, "ctx", axis=0, tiled=True),
    )
    segment_list = (
        lax.all_gather(local_part[0], "dp", axis=0, tiled=True),
        lax.all_gather(local_part[1], "dp", axis=0, tiled=True),
        lax.all_gather(local_part[2], "dp", axis=0, tiled=True),
        lax.all_gather(local_part[3], "dp", axis=0, tiled=True),
        lax.all_gather(local_part[4], "dp", axis=0, tiled=True),
    )
    flattened_query = jnp.dot(normed, segment_list[0], preferred_element_type=jnp.float32).astype(
        jnp.bfloat16
    )
    query_matrix = flattened_query.reshape(
        token_rows, KEY_VALUE_HEADS, query_group_count, HEAD_SIZE
    ).transpose(1, 2, 0, 3)
    key_matrix = (
        jnp.dot(normed, segment_list[1], preferred_element_type=jnp.float32)
        .astype(jnp.bfloat16)
        .reshape(token_rows, KEY_VALUE_HEADS, HEAD_SIZE)
    )
    value_matrix = (
        jnp.dot(normed, segment_list[2], preferred_element_type=jnp.float32)
        .astype(jnp.bfloat16)
        .reshape(token_rows, KEY_VALUE_HEADS, HEAD_SIZE)
    )
    marker_key_rows = jnp.dot(pooled, segment_list[3], preferred_element_type=jnp.float32).astype(
        jnp.bfloat16
    )
    marker_value_rows = jnp.dot(pooled, segment_list[4], preferred_element_type=jnp.float32).astype(
        jnp.bfloat16
    )
    raw_top, raw_sum, raw_weighted = raw_attention(
        query_matrix, key_matrix, value_matrix, begin_offset, length, score_scale
    )
    halved_rows = token_rows // 2
    first_q = query_matrix[:, :, :halved_rows]
    second_q = query_matrix[:, :, halved_rows:]
    empty_state = (
        jnp.full((KEY_VALUE_HEADS, query_group_count, halved_rows), negative_filler, jnp.float32),
        jnp.zeros((KEY_VALUE_HEADS, query_group_count, halved_rows), jnp.float32),
        jnp.zeros((KEY_VALUE_HEADS, query_group_count, halved_rows, HEAD_SIZE), jnp.float32),
    )
    segment_list = (
        lax.all_gather(marker_key_rows, "ctx", axis=0, tiled=True),
        lax.all_gather(marker_value_rows, "ctx", axis=0, tiled=True),
        lax.all_gather(live_slot.astype(jnp.bfloat16), "ctx", axis=0, tiled=True),
    )
    segment_keys = segment_list[0].reshape(-1, KEY_VALUE_HEADS, HEAD_SIZE)
    segment_values = segment_list[1].reshape(-1, KEY_VALUE_HEADS, HEAD_SIZE)
    first_state = beacon_update(
        empty_state,
        first_q,
        my_span,
        segment_keys,
        segment_values,
        segment_list[2],
        marker_slot_count,
        score_scale,
    )
    second_state = beacon_update(
        empty_state,
        second_q,
        my_span,
        segment_keys,
        segment_values,
        segment_list[2],
        marker_slot_count,
        score_scale,
    )
    first_state, second_state = (first_state, second_state)
    beacon_top = jnp.concatenate([first_state[0], second_state[0]], axis=2)
    beacon_sum = jnp.concatenate([first_state[1], second_state[1]], axis=2)
    beacon_weighted = jnp.concatenate([first_state[2], second_state[2]], axis=2)
    joint_top = jnp.maximum(raw_top, beacon_top)
    raw_factor = jnp.exp(raw_top - joint_top)
    beacon_factor = jnp.exp(beacon_top - joint_top)
    weight_sum = raw_sum * raw_factor + beacon_sum * beacon_factor
    weighted = raw_weighted * raw_factor[..., None] + beacon_weighted * beacon_factor[..., None]
    result = weighted / jnp.where(weight_sum > 0, weight_sum, 1.0)[..., None]
    result = result.transpose(2, 0, 1, 3).reshape(token_rows, QUERY_HEADS * HEAD_SIZE)
    valid = begin_offset + jnp.arange(token_rows, dtype=jnp.int32) < length
    result = jnp.where(valid[:, None], result, 0.0).astype(jnp.bfloat16)
    return result[None]


GROUP = QUERY_HEADS // KEY_VALUE_HEADS
PIECES = 4 + GROUP
GROUPS = (PIECES + 1) // 2
AHEAD = 5
Y_FIRST = (PIECES - 2, PIECES - 1)
FLOWS = [(p, 0) for p in range(PIECES)] + [(p, 1) for p in Y_FIRST]
STRIPS = 4
MESH = pl.DeviceIdType.MESH


def sublayer_kernel(
    n_dp,
    n_ctx,
    length_ref,
    level_ref,
    hidden_hbm,
    gain_ref,
    wq_ref,
    wk_ref,
    wv_ref,
    mk_ref,
    mv_ref,
    out_ref,
    hidden,
    levels,
    weights_buf,
    normed,
    pooled,
    beacons,
    live_bias,
    kv_buf,
    q_buf,
    span_bias,
    raw_bias,
    made_out,
    own_sem,
    load_sem,
    xs,
    xr,
    zu,
    zd,
    zr,
    ys,
    yr,
    cs,
    cr,
    hs,
    hr,
    ls,
    lr,
    bs,
    br,
    os_,
    or_,
    keep_sem,
):
    tokens = hidden_hbm.shape[0]
    rows = wq_ref.shape[0]
    slots = tokens // 4
    n_z = n_ctx // 2
    pair = 2 * slots
    dp = lax.axis_index("dp")
    ctx = lax.axis_index("ctx")
    z, x = ctx // 2, lax.rem(ctx, 2)
    other_x = 1 - x
    x_peer = (dp, z * 2 + other_x)
    y_dp = lax.rem(dp + n_dp // 2, n_dp)
    y_peer = (y_dp, ctx)
    mate = (dp + 1 - 2 * lax.rem(dp, 2), ctx)
    has_up, has_down = z + 1 < n_z, z > 0
    z_up = (dp, lax.rem(z + 1, n_z) * 2 + x)
    z_down = (dp, lax.rem(z + n_z - 1, n_z) * 2 + x)

    barrier = pltpu.get_barrier_semaphore()

    def greet(peer):
        pl.semaphore_signal(barrier, inc=1, device_id=peer, device_id_type=MESH)

    for peer in (x_peer, y_peer, mate):
        greet(peer)

    @pl.when(has_up)
    def _():
        greet(z_up)

    @pl.when(has_down)
    def _():
        greet(z_down)

    def remote(source, target, send, recv, peer):
        return pltpu.make_async_remote_copy(
            src_ref=source,
            dst_ref=target,
            send_sem=send,
            recv_sem=recv,
            device_id=peer,
            device_id_type=MESH,
        )

    strip = tokens // STRIPS

    def load_copy(i):
        part = pl.ds(i * strip, strip)
        return pltpu.make_async_copy(
            hidden_hbm.at[part, :], hidden.at[0, part, :], load_sem.at[i]
        )

    for i in range(STRIPS):
        load_copy(i).start()

    def piece_source(p, head):
        if p < 4:
            ref = (mk_ref, mv_ref, wk_ref, wv_ref)[p]
            column = head * HEAD_SIZE
        else:
            ref = wq_ref
            column = (head * GROUP + p - 4) * HEAD_SIZE
        return ref.at[:, pl.ds(pl.multiple_of(column, HEAD_SIZE), HEAD_SIZE)]

    def piece_rows(p, start, count):
        return weights_buf.at[
            p // 2,
            pl.ds(pl.multiple_of(start * rows, 16), count * rows),
            pl.ds((p % 2) * HEAD_SIZE, HEAD_SIZE),
        ]

    me = dp * n_ctx + ctx

    def amount(blocks):
        for a in range(1, GROUPS + 1):
            if blocks % (2 * a) == 0 and blocks // (2 * a) <= n_dp * n_ctx:
                return weights_buf.at[0:a, 0 : blocks // (2 * a) * rows, :]
        return weights_buf.at[0, 0 : blocks * rows, 0:HEAD_SIZE]

    def own_copy(p):
        return pltpu.make_async_copy(piece_source(p, x), piece_rows(p, me, 1), own_sem)

    def x_copy(p):
        return remote(piece_source(p, other_x), piece_rows(p, me, 1), xs, xr.at[p], x_peer)

    for p in range(PIECES):
        own_copy(p).start()

    for m in range(1, n_z):

        @pl.when(z < m)
        def _():
            beacons[m * pair : (m + 1) * pair, :] = jnp.zeros(
                (pair, 2 * HEAD_SIZE), jnp.bfloat16
            )
            live_bias[m] = jnp.full((8, pair), negative_filler, jnp.float32)

    levels[x] = jnp.broadcast_to(level_ref[0, 0], (8, 128))
    length = length_ref[0]

    pl.semaphore_wait(
        barrier, 3 + has_up.astype(jnp.int32) + has_down.astype(jnp.int32)
    )

    def z_copy(f, source, step):
        p, column = FLOWS[f]
        block = piece_rows(p, (dp, y_dp)[column] * n_ctx + source * 2, 2)
        sends = zu if step > 0 else zd
        peer = z_up if step > 0 else z_down
        return remote(block, block, sends, zr.at[f, source], peer)

    def y_copy(p, source):
        block = piece_rows(p, dp * n_ctx + source * 2, 2)
        return remote(block, block, ys, yr.at[p], y_peer)

    def c_copy(p, which):
        block = piece_rows(p, (dp, y_dp)[which] * n_ctx, n_ctx)
        return remote(block, block, cs, cr.at[p // 2], mate)

    def begin(p):
        x_copy(p).wait_recv()
        y_copy(p, z).start()

    def launch(f):
        p, column = FLOWS[f]
        if column == 1:
            y_copy(p, z).wait_recv()
        elif p not in Y_FIRST:
            begin(p)

        @pl.when(has_up)
        def _():
            z_copy(f, z, 1).start()

        @pl.when(has_down)
        def _():
            z_copy(f, z, -1).start()

    def relay(f, d):
        p, column = FLOWS[f]
        spread = column == 0 and p not in Y_FIRST

        @pl.when(z - d >= 0)
        def _():
            z_copy(f, z - d, 1).wait_recv()
            if spread:
                y_copy(p, z - d).start()

            @pl.when(has_up)
            def _():
                z_copy(f, z - d, 1).start()

        @pl.when(z + d < n_z)
        def _():
            z_copy(f, z + d, -1).wait_recv()
            if spread:
                y_copy(p, z + d).start()

            @pl.when(has_down)
            def _():
                z_copy(f, z + d, -1).start()

        if d == n_z - 1:
            c_copy(p, column).start()

    def tick(t):
        for d in range(1, n_z):
            f = t - d + 1
            if 0 <= f < len(FLOWS):
                relay(f, d)
        if t + AHEAD < len(FLOWS):
            launch(t + AHEAD)

    def y_arrived(p):
        if p not in Y_FIRST:
            block = piece_rows(p, y_dp * n_ctx, n_ctx)
            remote(block, block, ys, yr.at[p], y_peer).wait_recv()
            c_copy(p, 1).start()

    def arrived(g):
        last = HEAD_SIZE * (1 + min(1, PIECES - 1 - 2 * g))
        block = weights_buf.at[g, 0 : 2 * n_ctx * rows, 0:last]
        remote(block, block, cs, cr.at[g], mate).wait_recv()

    def hidden_copy(i):
        part = pl.ds(i * strip, strip)
        return remote(
            hidden_hbm.at[part, :], hidden.at[1, part, :], hs, hr.at[i], x_peer
        )

    level_copy = remote(levels.at[x], levels.at[x], ls, lr, x_peer)

    def beacon_rows(first, count):
        return beacons.at[pl.ds(pl.multiple_of(first * slots, slots), count * slots), :]

    def send_up(source, kind, level):
        for d in range(1, n_z):

            @pl.when(z + d < n_z)
            def _():
                peer = (dp, lax.rem(z + d, n_z) * 2 + x)
                remote(source, source, bs.at[kind], br.at[kind, level], peer).start()

    def head_columns(head, j):
        return pl.ds(pl.multiple_of((head * GROUP + j) * HEAD_SIZE, HEAD_SIZE), HEAD_SIZE)

    def out_copy(j):
        return remote(
            made_out.at[1, j], out_ref.at[:, head_columns(x, j)], os_, or_, x_peer
        )

    def keep_copy(j):
        return pltpu.make_async_copy(
            made_out.at[0, j], out_ref.at[:, head_columns(x, j)], keep_sem
        )

    def half(head):
        width = GROUP * HEAD_SIZE
        return out_ref.at[:, pl.ds(pl.multiple_of(head * width, HEAD_SIZE), width)]

    for p in range(PIECES):
        x_copy(p).start()
    level_copy.start()
    for i in range(STRIPS):
        hidden_copy(i).start()

    gain = gain_ref[...][None, :]

    def norm_strip(i, which, slot):
        def body(k, carry):
            part = pl.ds(pl.multiple_of(i * strip + k * 16, 16), 16)
            values = hidden[which, part, :].astype(jnp.float32)
            factor = lax.rsqrt(jnp.mean(values * values, axis=-1, keepdims=True) + eps_norm)
            normed[slot, part, :] = (values * factor * gain).astype(jnp.bfloat16)
            return carry

        lax.fori_loop(0, strip // 16, body, 0)

    def norm_own(i):
        load_copy(i).wait()
        norm_strip(i, 0, x)

    def norm_other(i):
        hidden_copy(i).wait_recv()
        norm_strip(i, 1, other_x)

    lane = lax.broadcasted_iota(jnp.int32, (1, pair), 1)
    slot_id = lax.rem(lane, slots)
    sub = lane // slots

    def stride_of(level):
        return jnp.where(
            level == 0, 4, jnp.where(level == 1, 8, jnp.where(level == 2, 16, 32))
        )

    def own_live():
        level = jnp.where(sub == 0, levels[0, 0:1, :], levels[1, 0:1, :])
        stride = stride_of(level)
        owner = 2 * z + sub
        live = (slot_id * stride < tokens) & (owner * tokens + slot_id * stride < length)
        live_bias[z] = jnp.broadcast_to(jnp.where(live, 0.0, negative_filler), (8, pair))
        send_up(live_bias.at[z], 1, z)

    def mask_far():
        for s in range(2):
            for m in range(n_z):
                seen = (2 * m + sub) < (2 * z + s)
                span_bias[s, :, m * pair : (m + 1) * pair] = jnp.where(
                    seen, live_bias[m], negative_filler
                )

    def mask_near():
        for s in range(2):
            row_id = lax.broadcasted_iota(jnp.int32, (tokens, tokens), 0)
            col_id = lax.broadcasted_iota(jnp.int32, (tokens, tokens), 1)
            seen = (col_id <= row_id) & ((z * 2 + s) * tokens + col_id < length)
            raw_bias[s] = jnp.where(seen, 0.0, negative_filler)

    def pool(s):
        span = z * 2 + s
        level = jnp.broadcast_to(levels[s, 0:1, :], (slots, 128))
        stride = stride_of(level)
        slot = lax.broadcasted_iota(jnp.int32, (slots, 128), 0)
        parts = []
        for b in range(tokens // 128):
            pos = lax.broadcasted_iota(jnp.int32, (slots, 128), 1) + b * 128
            inside = (
                (pos >= slot * stride)
                & (pos < (slot + 1) * stride)
                & (span * tokens + pos < length)
            )
            parts.append(jnp.where(inside, 1.0, 0.0))
        inside = jnp.concatenate(parts, axis=1)
        scale = 1.0 / jnp.maximum(jnp.sum(inside, axis=1, keepdims=True), 1.0)
        table = inside.astype(jnp.bfloat16)
        width = normed.shape[2] // 4

        def body(i, carry):
            cols = pl.ds(pl.multiple_of(i * width, 128), width)
            total = jnp.dot(table, normed[s, :, cols], preferred_element_type=jnp.float32)
            pooled[pl.ds(pl.multiple_of(s * slots, slots), slots), cols] = (
                total * scale
            ).astype(jnp.bfloat16)
            return carry

        lax.fori_loop(0, 4, body, 0)

    def project_kv(s):
        kv_buf[s] = jnp.dot(
            normed[s], weights_buf[1], preferred_element_type=jnp.float32
        ).astype(jnp.bfloat16)

    def project_query(s, g):
        result = jnp.dot(
            normed[s], weights_buf[g], preferred_element_type=jnp.float32
        ).astype(jnp.bfloat16)
        q_buf[s, 2 * (g - 2)] = result[:, :HEAD_SIZE]
        q_buf[s, 2 * (g - 2) + 1] = result[:, HEAD_SIZE:]

    def project_last(s):
        q_buf[s, GROUP - 1] = jnp.dot(
            normed[s], weights_buf[GROUPS - 1, :, :HEAD_SIZE], preferred_element_type=jnp.float32
        ).astype(jnp.bfloat16)

    def make_beacons(s):
        part = pl.ds(pl.multiple_of(s * slots, slots), slots)
        made = jnp.dot(pooled[part, :], weights_buf[0], preferred_element_type=jnp.float32)
        block = beacon_rows(z * 2 + s, 1)
        block[...] = made.astype(jnp.bfloat16)
        send_up(block, 0, z)

    def await_beacons():
        for m in range(n_z - 1):

            @pl.when(m < z)
            def _():
                block = beacon_rows(2 * m, 2)
                remote(block, block, bs.at[0], br.at[0, m], x_peer).wait_recv()
                bias = live_bias.at[m]
                remote(bias, bias, bs.at[1], br.at[1, m], x_peer).wait_recv()

        mask_far()

    factor = math.log2(math.e) / math.sqrt(HEAD_SIZE)
    contract = (((1,), (1,)), ((), ()))

    def attend(s, j, which, width, count):
        query = q_buf[s, pl.ds(j, count)].reshape(count * tokens, HEAD_SIZE)
        far = lax.dot_general(
            query, beacons[:width, :HEAD_SIZE], contract, preferred_element_type=jnp.float32
        )
        near = lax.dot_general(
            query, kv_buf[s, :, :HEAD_SIZE], contract, preferred_element_type=jnp.float32
        )
        far = far * factor + span_bias[s, 0:1, :width]
        near = (near * factor).reshape(count, tokens, tokens) + raw_bias[s][None]
        near = near.reshape(count * tokens, tokens)
        top = jnp.maximum(
            jnp.max(far, axis=1, keepdims=True), jnp.max(near, axis=1, keepdims=True)
        )
        far = jnp.exp2(far - top)
        near = jnp.exp2(near - top)
        total = jnp.sum(far, axis=1, keepdims=True) + jnp.sum(near, axis=1, keepdims=True)
        mixed = jnp.dot(
            far.astype(jnp.bfloat16),
            beacons[:width, HEAD_SIZE:],
            preferred_element_type=jnp.float32,
        ) + jnp.dot(
            near.astype(jnp.bfloat16),
            kv_buf[s, :, HEAD_SIZE:],
            preferred_element_type=jnp.float32,
        )
        row = lax.broadcasted_iota(jnp.int32, (count, tokens, 1), 1)
        position = (z * 2 + s) * tokens + row.reshape(count * tokens, 1)
        scale = jnp.where(position < length, 1.0 / total, 0.0)
        made_out[which, pl.ds(j, count)] = (
            (mixed * scale).astype(jnp.bfloat16).reshape(count, tokens, HEAD_SIZE)
        )

    def heads(first, last):
        count = last - first
        for which, s in ((1, other_x), (0, x)):

            @pl.when(z == 0)
            def _():
                attend(s, first, which, pair, count)

            @pl.when(z > 0)
            def _():
                attend(s, first, which, n_z * pair, count)

            for j in range(first, last):
                (keep_copy, out_copy)[which](j).start()

    pltpu.make_async_copy(amount(PIECES), amount(PIECES), own_sem).wait()
    for f in range(AHEAD):
        launch(f)
    for i in range(STRIPS):
        norm_own(i)
    for p in Y_FIRST:
        begin(p)
    tick(0)
    pool(x)
    mask_near()
    tick(1)
    tick(2)
    norm_other(0)
    tick(3)
    tick(4)
    level_copy.wait_recv()
    own_live()
    tick(5)
    y_arrived(0)
    norm_other(1)
    tick(6)
    y_arrived(1)
    arrived(0)
    make_beacons(x)
    tick(7)
    y_arrived(2)
    tick(8)
    y_arrived(3)
    norm_other(2)
    arrived(1)
    project_kv(x)
    tick(9)
    y_arrived(4)
    tick(10)
    y_arrived(5)
    arrived(2)
    project_query(x, 2)
    tick(11)
    y_arrived(6)
    norm_other(3)
    pool(other_x)
    make_beacons(other_x)
    project_kv(other_x)
    tick(12)
    y_arrived(7)
    project_query(other_x, 2)
    arrived(3)
    project_query(x, 3)
    project_query(other_x, 3)
    tick(13)
    y_arrived(8)
    await_beacons()
    heads(0, 2)
    tick(14)
    heads(2, 4)
    arrived(4)
    project_query(x, 4)
    project_query(other_x, 4)
    heads(4, 6)
    arrived(5)
    project_last(x)
    project_last(other_x)
    heads(6, 7)
    pltpu.make_async_copy(half(x), half(x), keep_sem).wait()
    remote(half(other_x), half(other_x), os_, or_, x_peer).wait()
    remote(amount(PIECES), amount(PIECES), xs, xr.at[0], x_peer).wait_send()
    every = amount((PIECES - len(Y_FIRST)) * 2 * n_z + 2 * len(Y_FIRST))
    remote(every, every, ys, yr.at[0], y_peer).wait_send()
    every = amount(PIECES * 2 * n_ctx)
    remote(every, every, cs, cr.at[0], mate).wait_send()
    for m in range(n_z):

        @pl.when(has_up & (z == m))
        def _():
            every = amount(len(FLOWS) * 2 * (m + 1))
            remote(every, every, zu, zr.at[0, 0], z_up).wait_send()
            every = beacons.at[0 : (n_z - 1 - m) * pair, :]
            remote(every, every, bs.at[0], br.at[0, 0], z_up).wait_send()
            every = live_bias.at[0 : n_z - 1 - m]
            remote(every, every, bs.at[1], br.at[1, 0], z_up).wait_send()

        @pl.when(has_down & (z == m))
        def _():
            every = amount(len(FLOWS) * 2 * (n_z - m))
            remote(every, every, zd, zr.at[0, 0], z_down).wait_send()

    remote(hidden_hbm, hidden.at[1], hs, hr.at[0], x_peer).wait_send()
    level_copy.wait_send()


def on_device_paired(
    n_dp,
    n_ctx,
    hidden_in,
    norm_gain,
    w_query,
    w_key,
    value_weight,
    marker_key_weight,
    marker_value_weight,
    ratio_level,
    hist_len,
):
    tokens, width = hidden_in.shape[1:]
    slots = tokens // 4
    n_z = n_ctx // 2
    flows = len(FLOWS)
    dma = pltpu.SemaphoreType.DMA
    vmem = pl.BlockSpec(memory_space=pltpu.VMEM)
    smem = pl.BlockSpec(memory_space=pltpu.SMEM)
    hbm = pl.BlockSpec(memory_space=pl.ANY)
    bf16 = jnp.bfloat16
    result = pl.pallas_call(
        functools.partial(sublayer_kernel, n_dp, n_ctx),
        out_shape=jax.ShapeDtypeStruct((tokens, QUERY_HEADS * HEAD_SIZE), bf16),
        in_specs=[smem, smem, hbm, vmem] + [hbm] * 5,
        out_specs=hbm,
        scratch_shapes=[
            pltpu.VMEM((2, tokens, width), bf16),
            pltpu.VMEM((2, 8, 128), jnp.int32),
            pltpu.VMEM((GROUPS, width, 2 * HEAD_SIZE), bf16),
            pltpu.VMEM((2, tokens, width), bf16),
            pltpu.VMEM((2 * slots, width), bf16),
            pltpu.VMEM((n_ctx * slots, 2 * HEAD_SIZE), bf16),
            pltpu.VMEM((n_z, 8, 2 * slots), jnp.float32),
            pltpu.VMEM((2, tokens, 2 * HEAD_SIZE), bf16),
            pltpu.VMEM((2, GROUP, tokens, HEAD_SIZE), bf16),
            pltpu.VMEM((2, 8, n_ctx * slots), jnp.float32),
            pltpu.VMEM((2, tokens, tokens), jnp.float32),
            pltpu.VMEM((2, GROUP, tokens, HEAD_SIZE), bf16),
            dma,
            dma((STRIPS,)),
            dma,
            dma((PIECES,)),
            dma,
            dma,
            dma((flows, n_z)),
            dma,
            dma((PIECES,)),
            dma,
            dma((GROUPS,)),
            dma,
            dma((STRIPS,)),
            dma,
            dma,
            dma((2,)),
            dma((2, n_z)),
            dma,
            dma,
            dma,
        ],
        compiler_params=pltpu.CompilerParams(
            collective_id=0, has_side_effects=True, vmem_limit_bytes=56 * 2**20
        ),
    )(
        hist_len,
        ratio_level,
        hidden_in[0],
        norm_gain,
        w_query,
        w_key,
        value_weight,
        marker_key_weight,
        marker_value_weight,
    )
    return result[None]


def solution(mesh):
    n_dp, n_ctx = mesh.shape["dp"], mesh.shape["ctx"]

    def body(*args):
        tokens, rows = args[0].shape[1], args[2].shape[0]
        if rows % 16 == 0 and tokens == 256 and n_dp == 4 and n_ctx % 2 == 0 and n_ctx > 2:
            return on_device_paired(n_dp, n_ctx, *args)
        return on_device(*args)

    return jax.shard_map(
        body,
        mesh=mesh,
        in_specs=(
            P("dp", "ctx", None),
            P(),
            P(("dp", "ctx"), None),
            P(("dp", "ctx"), None),
            P(("dp", "ctx"), None),
            P(("dp", "ctx"), None),
            P(("dp", "ctx"), None),
            P("dp", "ctx"),
            P("dp"),
        ),
        out_specs=P("dp", "ctx", None),
        check_vma=False,
    )
```
